256 devices in a mesh: grp: 8 (over z_hi, y), row: 32 (over z_lo, x, core).
Axes of the slice: x: 4, y: 4, z: 8 (z_hi: 2, z_lo: 4; z = z_hi * 4 + z_lo), core: 2. Of those that a mesh axis runs over, the one named last changes fastest.
Arguments:
- points: bfloat16 [524288, 128], P(('grp', 'row')), as said below
- centers: bfloat16 [8192, 128], replicated, as said below
- inner_factor: bfloat16 [8192, 8192], P('row'), as said below
- outer_factor: bfloat16 [8192, 8192], P('row'), as said below
- iterate: float32 [64, 8192], P(None, 'row'), may hold values from -6 to 6
- residual: float32 [64, 8192], P(None, 'row'), as said below
- direction: float32 [64, 8192], P(None, 'row'), as said below
Outputs:
- next_iterate: float32 [64, 8192], P(None, 'row')
- next_residual: float32 [64, 8192], P(None, 'row')
- next_direction: float32 [64, 8192], P(None, 'row')
The draws below stay inside these ranges and needn't reach their ends.
Inputs may be any that keep to these rules, and one draw needn't show every extreme that they name: `inner_factor`: upper triangular: zero below the diagonal, positive on it. `outer_factor`: upper triangular: zero below the diagonal, positive on it. `residual`: finite real values. `direction`: finite real values. `points`: finite real values. `centers`: finite real values.
All inputs are finite; a program needn't handle non-finite values.
Results may differ from the reference program's by a relative error of at most 0.0056.
Values may be sent and summed in bfloat16 or wider, within the bound.
No kernel may reach another device: no remote copies, remote signals or barrier semaphores. Data moves between devices by JAX's collectives and lax.ppermute only.
A program may use at most 64 MiB of HBM per device.

```python
import math
import jax
import jax.numpy as jnp
from jax import lax

D = 128
M = 8192
R = 64
N_DEV = 2048
NPTS = 524288


def upper_factor(key, lowest, highest, spread):
    key_diag, key_off = jax.random.split(key)
    position = jnp.arange(M)
    above = position[None, :] > position[:, None]
    on_diag = position[None, :] == position[:, None]
    off_values = jax.random.uniform(key_off, (M, M), jnp.float32, -1.0, 1.0) * (spread * math.sqrt(3.0 / M))
    diag_values = jnp.exp(jax.random.uniform(key_diag, (M,), jnp.float32, math.log(lowest), math.log(highest)))
    filled = jnp.where(above, off_values, 0.0)
    return jnp.where(on_diag, diag_values[:, None], filled)


def draw_inner_factor(key, part):
    return upper_factor(jax.random.fold_in(key, 11), 1.0, 3.0, 1.0).astype(jnp.bfloat16)


def draw_outer_factor(key, part):
    return upper_factor(jax.random.fold_in(key, 12), 100.0, 400.0, 120.0).astype(jnp.bfloat16)


def point_cloud(key):
    key_center, key_noise, key_owner, key_scale, key_shift = jax.random.split(jax.random.fold_in(key, 31), 5)
    center_values = jnp.clip(jax.random.normal(key_center, (M, D), jnp.float32), -6.0, 6.0)
    shift_values = jnp.clip(jax.random.normal(key_shift, (M, D), jnp.float32), -6.0, 6.0) * 0.2
    device_count = NPTS // N_DEV
    span = max(M * N_DEV // NPTS, 1)
    index = jnp.arange(NPTS, dtype=jnp.int32)
    device = index // N_DEV
    local_owner = jax.random.randint(key_owner, (NPTS,), 0, span, dtype=jnp.int32)
    owner = (device * M // device_count + local_owner).astype(jnp.int32)
    point_scale = jnp.exp(jax.random.uniform(key_scale, (NPTS, 1), jnp.float32, math.log(0.05), math.log(0.7)))
    noise = jnp.clip(jax.random.normal(key_noise, (NPTS, D), jnp.float32), -6.0, 6.0) * point_scale
    point_values = center_values[owner] + shift_values[owner] + noise
    return (center_values, point_values)


def draw_centers(key, part):
    return point_cloud(key)[0].astype(jnp.bfloat16)


def draw_points(key, part):
    return point_cloud(key)[1].astype(jnp.bfloat16)


def scaled_state(key):
    key_base, key_row, key_col = jax.random.split(key, 3)
    position = jnp.arange(M).astype(jnp.float32) / max(M - 1, 1)
    base = jax.random.normal(key_base, (R, M), jnp.float32)
    row_scale = jnp.exp(jax.random.uniform(key_row, (M,), jnp.float32, math.log(0.3), math.log(3.0)))
    ramp = 1.0 + (math.sqrt(3.0) - 1.0) * position
    col_scale = jnp.exp(jax.random.uniform(key_col, (R,), jnp.float32, math.log(0.3), math.log(3.0)))
    return base * (row_scale * ramp)[None, :] * col_scale[:, None]


def draw_residual(key, part):
    return scaled_state(jax.random.fold_in(key, 21)).astype(jnp.float32)


def draw_direction(key, part):
    return scaled_state(jax.random.fold_in(key, 22)).astype(jnp.float32)


def shard_levels(key, dims, cuts, low, largest):
    def one(dim, shards_of):
        heights = jax.random.uniform(jax.random.fold_in(jax.random.fold_in(key, 6), dim), (shards_of,), jnp.float32, low / len(cuts), largest / len(cuts))
        return jnp.repeat(jnp.exp(heights), dims[dim] // shards_of).reshape((-1,) + (1,) * (len(dims) - dim - 1))

    gain = one(*cuts[0])
    for cut in cuts[1:]:
        gain = gain * one(*cut)
    return gain


def gaussian(stream_key, dims, scale, reach, cuts=(), held_as=jnp.bfloat16):
    drawn = scale * jax.random.normal(stream_key, dims, jnp.float32)
    if cuts:
        drawn = drawn * shard_levels(stream_key, dims, cuts, -0.22, 0.18)
    return jnp.clip(drawn, -reach, reach).astype(held_as)


def setup_inputs(seed: int = 0) -> dict:
    key_of = jax.random.split(jax.random.key(seed), 8)
    return {
        "points": draw_points(jax.random.fold_in(key_of[7], 71), 0),
        "centers": draw_centers(jax.random.fold_in(key_of[7], 71), 0),
        "inner_factor": draw_inner_factor(jax.random.fold_in(key_of[7], 71), 0),
        "outer_factor": draw_outer_factor(jax.random.fold_in(key_of[7], 71), 0),
        "iterate": gaussian(key_of[4], (R, M), 1.0, 6.0, ((1, 32),), jnp.float32),
        "residual": draw_residual(jax.random.fold_in(key_of[7], 71), 0),
        "direction": draw_direction(jax.random.fold_in(key_of[7], 71), 0),
    }


ridge_weight = 0.5


def kernel_rows(block_points, centers, center_norms):
    point_wide = block_points.astype(jnp.float32)
    point_norms = jnp.sum(point_wide * point_wide, axis=1)
    cross_term = lax.dot_general(block_points, centers, (((1,), (1,)), ((), ())), preferred_element_type=jnp.float32)
    distance = point_norms[:, None] + center_norms[None, :] - 2.0 * cross_term
    return jnp.exp(distance * (-4.0 / D)).astype(jnp.bfloat16)


def reference(points, centers, inner_factor, outer_factor, iterate, residual, direction):
    contract_last = (((1,), (1,)), ((), ()))
    direction_half = direction.astype(jnp.bfloat16)
    inner_term = lax.dot_general(direction_half, inner_factor, contract_last, preferred_element_type=jnp.float32)
    inner_half = inner_term.astype(jnp.bfloat16)
    outer_half = lax.dot_general(inner_half, outer_factor, contract_last, preferred_element_type=jnp.float32).astype(jnp.bfloat16)
    center_wide = centers.astype(jnp.float32)
    center_norms = jnp.sum(center_wide * center_wide, axis=1)
    block_rows = math.gcd(NPTS, 4096)
    point_blocks = points.reshape(NPTS // block_rows, block_rows, D)

    def one_block(carried, block_points):
        kernel_block = kernel_rows(block_points, centers, center_norms)
        fitted = lax.dot_general(outer_half, kernel_block, contract_last, preferred_element_type=jnp.float32).astype(jnp.bfloat16)
        return carried + jnp.dot(fitted, kernel_block, preferred_element_type=jnp.float32), None

    normal_eq, _ = lax.scan(one_block, jnp.zeros((R, M), jnp.float32), point_blocks)
    normal_half = normal_eq.astype(jnp.bfloat16)
    shaped = jnp.dot(normal_half, outer_factor, preferred_element_type=jnp.float32) / NPTS + ridge_weight * inner_term
    shaped_half = shaped.astype(jnp.bfloat16)
    operator_image = jnp.dot(shaped_half, inner_factor, preferred_element_type=jnp.float32)
    old_norm = jnp.sum(residual * residual, axis=1)
    curvature = jnp.sum(direction * operator_image, axis=1)
    step_size = (old_norm / curvature)[:, None]
    next_iterate = iterate + step_size * direction
    next_residual = residual - step_size * operator_image
    new_norm = jnp.sum(next_residual * next_residual, axis=1)
    next_direction = next_residual + (new_norm / old_norm)[:, None] * direction
    return (next_iterate, next_residual, next_direction)
```

```python
import functools
import jax
import jax.numpy as jnp
from jax import lax
from jax.sharding import Mesh, PartitionSpec as P
from jax.experimental import pallas as pl
from jax.experimental.pallas import tpu as pltpu

ridge_weight = 0.5
bf16, f32 = jnp.bfloat16, jnp.float32
ROW = ("zl", "x", "c")
GRP = ("zh", "y")
CHIPS = ("zh", "y", "zl", "x")
ALL = GRP + ROW
LAST = (((1,), (1,)), ((), ()))
VM = pl.BlockSpec(memory_space=pltpu.VMEM)
SM = pl.BlockSpec(memory_space=pltpu.SMEM)


def call(body, outs, args, specs=None, scratch=(), vmem=None, name=None):
    return pl.pallas_call(
        body,
        out_shape=outs,
        in_specs=specs or [VM] * len(args),
        out_specs=jax.tree.map(lambda _: VM, outs),
        scratch_shapes=scratch,
        compiler_params=pltpu.CompilerParams(vmem_limit_bytes=vmem),
        name=name,
    )(*args)


def sds(shape, dtype):
    return jax.ShapeDtypeStruct(shape, dtype)


def exchange(v, axes):
    return lax.all_to_all(v, axes, 0, 0, tiled=True)


def prep_body(g_ref, d_ref, out_ref):
    d = d_ref[pl.ds(pl.multiple_of(g_ref[0] * 8, 8), 8), :]
    hi = d.astype(bf16)
    lo = (d - hi.astype(f32)).astype(bf16)
    both = jnp.concatenate([hi, lo], axis=0)
    for r in range(out_ref.shape[0]):
        out_ref[r] = both


def rows_dot(x_ref, f_ref):
    acc = None
    for r in range(x_ref.shape[0]):
        part = lax.dot_general(
            x_ref[r], f_ref[:, r * 256 : (r + 1) * 256], LAST, preferred_element_type=f32
        )
        acc = part if acc is None else acc + part
    return acc


def inner_body(x_ref, f_ref, term_ref, full_ref, out_ref):
    acc = rows_dot(x_ref, f_ref)
    term_ref[...] = acc[:8]
    full_ref[...] = acc[:8] + acc[8:]
    half = acc[:8].astype(bf16)
    for r in range(out_ref.shape[0]):
        out_ref[r] = half


def outer_body(x_ref, f_ref, out_ref):
    half = rows_dot(x_ref, f_ref).astype(bf16)
    for r in range(out_ref.shape[0]):
        out_ref[r] = half


def pieces(rows, lane):
    wide = rows.astype(f32)
    norm = jnp.sum(wide * wide, axis=1, keepdims=True) * -0.5
    one = norm.astype(bf16).astype(f32)
    two = (norm - one).astype(bf16).astype(f32)
    three = norm - one - two
    return one, two, three


def with_norms(rows, first):
    lane = lax.broadcasted_iota(jnp.int32, rows.shape, 1)
    one, two, three = pieces(rows, lane)
    a, b = (0, 3) if first else (3, 0)
    extra = jnp.where(
        lane == a, one, jnp.where(lane == a + 1, two, jnp.where(lane == a + 2, three, 0.0))
    )
    extra = jnp.where((lane >= b) & (lane < b + 3), 1.0, extra)
    return jnp.concatenate([rows, extra.astype(bf16)], axis=1)


def kernel_body(c_ref, p_ref, cen_ref, w_ref, own_ref, oth_ref, k_ref, pa_ref, fit_ref):
    points = p_ref.shape[0]
    step = 256
    chunks = k_ref.shape[0]
    fit_ref[...] = jnp.zeros_like(fit_ref)
    for i in range(points // step):
        rows = pl.ds(i * step, step)
        pa_ref[rows, :] = with_norms(p_ref[rows, :], True)

    def first(j, carry):
        ca = with_norms(cen_ref[pl.ds(pl.multiple_of(j * 256, 256), 256), :], False)
        w = w_ref[j % 2, :, j // 2, :, :].reshape(64, 256)
        for i in range(points // step):
            rows = pl.ds(i * step, step)
            d = lax.dot_general(pa_ref[rows, :], ca, LAST, preferred_element_type=f32)
            k = jnp.exp(d * (8.0 / 128.0)).astype(bf16)
            k_ref[j, rows, :] = k
            fit_ref[:, rows] += lax.dot_general(w, k, LAST, preferred_element_type=f32)
        return carry

    lax.fori_loop(0, chunks, first, 0)
    fitted = fit_ref[...].astype(bf16)
    c = c_ref[0]

    def second(z, carry):
        for which, ref in ((0, own_ref), (1, oth_ref)):
            j = z * 2 + (c if which == 0 else 1 - c)
            n = jnp.dot(fitted, k_ref[j], preferred_element_type=f32)
            ref[:, z, :, :] = n.reshape(8, 8, 256).astype(ref.dtype)
        return carry

    lax.fori_loop(0, chunks // 2, second, 0)


def add_body(a_ref, b_ref, out_ref):
    out_ref[...] = (a_ref[...] + b_ref[...].astype(f32)).astype(out_ref.dtype)


def sum_blocks(ref, lanes=None):
    parts = [
        (ref[r] if lanes is None else ref[r, :, lanes[0] : lanes[1]]).astype(f32)
        for r in range(ref.shape[0])
    ]
    while len(parts) > 1:
        parts = [a + b for a, b in zip(parts[::2], parts[1::2])]
    return parts[0]


def back_outer_body(x_ref, f_ref, out_ref):
    half = sum_blocks(x_ref).astype(bf16)
    for r in range(out_ref.shape[0]):
        out_ref[r] = jnp.dot(half, f_ref[:, r * 256 : (r + 1) * 256], preferred_element_type=f32)


def back_inner_body(count, g_ref, x_ref, f_ref, term_ref, full_ref, res_ref, out_ref):
    shaped = sum_blocks(x_ref) / count + ridge_weight * term_ref[...]
    half = shaped.astype(bf16)
    curve = jnp.sum(half.astype(f32) * full_ref[...], axis=1, keepdims=True)
    res = res_ref[pl.ds(pl.multiple_of(g_ref[0] * 8, 8), 8), :]
    old = jnp.sum(res * res, axis=1, keepdims=True)
    lane = lax.broadcasted_iota(jnp.int32, (8, 128), 1)
    extra = jnp.where(lane == 0, curve, old)
    for r in range(out_ref.shape[0]):
        out_ref[r, :, :256] = jnp.dot(
            half, f_ref[:, r * 256 : (r + 1) * 256], preferred_element_type=f32
        )
        out_ref[r, :, 256:] = extra


def step_body(g_ref, x_ref, res_ref, keep_ref, out_ref):
    image = sum_blocks(x_ref, (0, 256))
    extra = sum_blocks(x_ref, (256, 384))
    curve, old = extra[:, 0:1], extra[:, 1:2]
    alpha = old / curve
    res = res_ref[pl.ds(pl.multiple_of(g_ref[0] * 8, 8), 8), :]
    new = res - alpha * image
    keep_ref[:, :256] = new
    lane = lax.broadcasted_iota(jnp.int32, (8, 128), 1)
    keep_ref[:, 256:] = jnp.where(lane == 0, alpha, old)
    part = jnp.broadcast_to(jnp.sum(new * new, axis=1, keepdims=True), (8, 128))
    for r in range(out_ref.shape[0]):
        out_ref[r] = part


def beta_body(x_ref, keep_ref, out_ref):
    total = sum_blocks(x_ref)
    new, extra = keep_ref[:, :256], keep_ref[:, 256:]
    lane = lax.broadcasted_iota(jnp.int32, (8, 128), 1)
    beta = total[:, 0:1] / extra[:, 1:2]
    extra = jnp.where(lane == 0, extra, beta)
    for r in range(out_ref.shape[0]):
        out_ref[r, :, :256] = new
        out_ref[r, :, 256:] = extra


def final_body(x_ref, it_ref, d_ref, ni_ref, nr_ref, nd_ref):
    for g in range(x_ref.shape[0]):
        rows = slice(g * 8, g * 8 + 8)
        new = x_ref[g, :, :256]
        alpha = x_ref[g, :, 256:257]
        beta = x_ref[g, :, 257:258]
        d = d_ref[rows, :]
        ni_ref[rows, :] = it_ref[rows, :] + alpha * d
        nr_ref[rows, :] = new
        nd_ref[rows, :] = new + beta * d


def local(points, centers, inner_factor, outer_factor, iterate, residual, direction):
    g = (lax.axis_index("zh") * 4 + lax.axis_index("y")).reshape(1)
    c = lax.axis_index("c").reshape(1)
    count = float(points.shape[0] * 256)
    x = call(prep_body, sds((32, 16, 256), bf16), (g, direction), [SM, VM], name="prep")
    x = exchange(x, ROW)
    term, full, x = call(
        inner_body,
        (sds((8, 256), f32), sds((8, 256), f32), sds((32, 8, 256), bf16)),
        (x, inner_factor),
        name="inner",
    )
    x = exchange(x, ROW)
    x = call(outer_body, sds((128, 8, 256), bf16), (x, outer_factor), name="outer")
    x = exchange(x, CHIPS)
    w = lax.all_gather(x, "c", axis=0, tiled=False).reshape(2, 8, 16, 8, 256)
    own, other = call(
        kernel_body,
        (sds((8, 16, 8, 256), f32), sds((8, 16, 8, 256), f32)),
        (c, points, centers, w),
        [SM, VM, VM, VM],
        scratch=[
            pltpu.VMEM((32, points.shape[0], 256), bf16),
            pltpu.VMEM((points.shape[0], 256), bf16),
            pltpu.VMEM((64, points.shape[0]), f32),
        ],
        vmem=56 * 1024 * 1024,
        name="kernel",
    )
    other = lax.ppermute(other, "c", [(0, 1), (1, 0)])
    x = call(add_body, sds((8, 16, 8, 256), bf16), (own, other), name="add")
    x = exchange(x.reshape(128, 8, 256), CHIPS)
    x = call(back_outer_body, sds((32, 8, 256), f32), (x, outer_factor), name="back_outer")
    x = exchange(x, ROW)
    x = call(
        functools.partial(back_inner_body, count),
        sds((32, 8, 384), f32),
        (g, x, inner_factor, term, full, residual),
        [SM] + [VM] * 5,
        name="back_inner",
    )
    x = exchange(x, ROW)
    keep, x = call(
        step_body,
        (sds((8, 384), f32), sds((32, 8, 128), f32)),
        (g, x, residual),
        [SM, VM, VM],
        name="step",
    )
    x = exchange(x, ROW)
    x = call(beta_body, sds((8, 8, 384), f32), (x, keep), name="beta")
    x = exchange(x, GRP)
    out = sds((64, 256), f32)
    return call(final_body, (out, out, out), (x, iterate, direction), name="final")


def solution(mesh):
    fine = Mesh(mesh.devices.reshape(2, 4, 4, 4, 2), ("zh", "y", "zl", "x", "c"))
    placed = (
        P(ALL, None),
        P(),
        P(ROW, None),
        P(ROW, None),
        P(None, ROW),
        P(None, ROW),
        P(None, ROW),
    )
    return jax.shard_map(
        local,
        mesh=fine,
        in_specs=placed,
        out_specs=(P(None, ROW),) * 3,
        check_vma=False,
    )
```

```python
import functools
import jax
import jax.numpy as jnp
from jax import lax
from jax.sharding import Mesh, PartitionSpec as P
from jax.experimental import pallas as pl
from jax.experimental.pallas import tpu as pltpu

ridge_weight = 0.5
bf16, f32 = jnp.bfloat16, jnp.float32
ROW = ("zl", "x", "c")
GRP = ("zh", "y")
CHIPS = ("zh", "y", "zl", "x")
ALL = GRP + ROW
SWAP = [(0, 1), (1, 0)]
LOG2E = 1.4426950408889634
MIB = 1024 * 1024
LAST = (((1,), (1,)), ((), ()))
VM = pl.BlockSpec(memory_space=pltpu.VMEM)
SM = pl.BlockSpec(memory_space=pltpu.SMEM)


def call(body, outs, args, specs=None, scratch=(), vmem=16, name=None):
    return pl.pallas_call(
        body,
        out_shape=outs,
        in_specs=specs or [VM] * len(args),
        out_specs=jax.tree.map(lambda _: VM, outs),
        scratch_shapes=scratch,
        compiler_params=pltpu.CompilerParams(vmem_limit_bytes=vmem * MIB),
        name=name,
    )(*args)


def sds(shape, dtype):
    return jax.ShapeDtypeStruct(shape, dtype)


def exchange(v, axes):
    return lax.all_to_all(v, axes, 0, 0, tiled=True)


def prep_body(g_ref, d_ref, out_ref):
    d = d_ref[pl.ds(pl.multiple_of(g_ref[0] * 8, 8), 8), :]
    hi = d.astype(bf16)
    lo = (d - hi.astype(f32)).astype(bf16)
    both = jnp.concatenate([hi, lo], axis=0)
    for r in range(out_ref.shape[0]):
        out_ref[r] = both


def rows_dot(x_ref, f_ref):
    acc = None
    for r in range(x_ref.shape[0]):
        part = lax.dot_general(
            x_ref[r], f_ref[:, r * 256 : (r + 1) * 256], LAST, preferred_element_type=f32
        )
        acc = part if acc is None else acc + part
    return acc


def inner_body(x_ref, f_ref, term_ref, full_ref, out_ref):
    acc = rows_dot(x_ref, f_ref)
    term_ref[...] = acc[:8]
    full_ref[...] = acc[:8] + acc[8:]
    half = acc[:8].astype(bf16)
    for r in range(out_ref.shape[0]):
        out_ref[r] = half


def outer_body(x_ref, f_ref, out_ref):
    half = rows_dot(x_ref, f_ref).astype(bf16)
    for r in range(out_ref.shape[0]):
        out_ref[r] = half


def norm_lanes(rows, first):
    wide = rows.astype(f32)
    lane = lax.broadcasted_iota(jnp.int32, (1, 128), 1)
    norm = jnp.sum(wide * wide, axis=1, keepdims=True) * -0.5
    one = norm.astype(bf16).astype(f32)
    rest = norm - one
    two = rest.astype(bf16).astype(f32)
    three = rest - two
    a, b = (0, 3) if first else (3, 0)
    ones = jnp.where((lane >= b) & (lane < b + 3), 1.0, 0.0)
    out = jnp.where(lane == a + 2, three, ones)
    out = jnp.where(lane == a + 1, two, out)
    return jnp.where(lane == a, one, out).astype(bf16)


def kernel_body(
    c_ref, p_ref, cen_ref, wo_ref, wx_ref, own_ref, oth_ref,
    k_ref, pa_ref, ca_ref, fit_ref, even_ref, odd_ref,
):
    nz = k_ref.shape[0]
    step = 256
    parts = p_ref.shape[0] // step
    c = c_ref[0]
    fit_ref[...] = jnp.zeros_like(fit_ref)
    pa_ref[:, :128] = p_ref[...]
    for i in range(parts):
        rows = pl.ds(i * step, step)
        pa_ref[rows, 128:] = norm_lanes(p_ref[rows, :], True)

    def load(z, slot):
        for h in range(2):
            start = pl.multiple_of((z * 2 + (c if h == 0 else 1 - c)) * 256, 256)
            block = cen_ref[pl.ds(start, 256), :]
            ca_ref[slot, h * 256 : h * 256 + 256, :128] = block
            ca_ref[slot, h * 256 : h * 256 + 256, 128:] = norm_lanes(block, False)

    def fill(z, slot, buf, i):
        rows = pl.ds(i * step, step)
        for h in range(2):
            cols = slice(h * 256, h * 256 + 256)
            d = lax.dot_general(
                pa_ref[rows, :], ca_ref[slot, cols, :], LAST, preferred_element_type=f32
            )
            k = jnp.exp2(d * (LOG2E * 8.0 / 128.0)).astype(bf16)
            k_ref[z, rows, cols] = k
            buf[rows, cols] = k

    def weights(z):
        own = wo_ref[:, z, :, :].reshape(64, 256)
        return jnp.concatenate([own, wx_ref[:, z, :, :].reshape(64, 256)], axis=1)

    def fit(w, buf, i):
        rows = pl.ds(i * step, step)
        fit_ref[rows, :] += lax.dot_general(buf[rows, :], w, LAST, preferred_element_type=f32)

    load(0, 0)
    load(1, 1)
    for i in range(parts):
        fill(0, 0, even_ref, i)

    def pair(h, carry):
        z = 2 * h + 1
        w = weights(z - 1)
        for i in range(parts):
            fit(w, even_ref, i)
            fill(z, 1, odd_ref, i)
        load(z + 1, 0)
        w = weights(z)
        for i in range(parts):
            fit(w, odd_ref, i)
            fill(z + 1, 0, even_ref, i)
        load(z + 2, 1)
        return carry

    lax.fori_loop(0, nz // 2 - 1, pair, 0)
    w = weights(nz - 2)
    for i in range(parts):
        fit(w, even_ref, i)
        fill(nz - 1, 1, odd_ref, i)
    w = weights(nz - 1)
    for i in range(parts):
        fit(w, odd_ref, i)
    fitted = fit_ref[...].T.astype(bf16)

    def second(z, carry):
        for h, ref in ((0, own_ref), (1, oth_ref)):
            n = jnp.dot(fitted, k_ref[z, :, h * 256 : h * 256 + 256], preferred_element_type=f32)
            ref[:, z, :, :] = n.reshape(8, 8, 256).astype(ref.dtype)
        return carry

    lax.fori_loop(0, nz, second, 0, unroll=2)


def add_body(a_ref, b_ref, out_ref):
    out_ref[...] = (a_ref[...] + b_ref[...].astype(f32)).astype(out_ref.dtype)


def sum_blocks(ref, lanes=None):
    parts = [
        (ref[r] if lanes is None else ref[r, :, lanes[0] : lanes[1]]).astype(f32)
        for r in range(ref.shape[0])
    ]
    while len(parts) > 1:
        parts = [a + b for a, b in zip(parts[::2], parts[1::2])]
    return parts[0]


def back_outer_body(x_ref, f_ref, out_ref):
    half = sum_blocks(x_ref).astype(bf16)
    for r in range(out_ref.shape[0]):
        out_ref[r] = jnp.dot(half, f_ref[:, r * 256 : (r + 1) * 256], preferred_element_type=f32)


def back_inner_body(count, g_ref, x_ref, f_ref, term_ref, full_ref, res_ref, out_ref):
    shaped = sum_blocks(x_ref) / count + ridge_weight * term_ref[...]
    half = shaped.astype(bf16)
    curve = jnp.sum(half.astype(f32) * full_ref[...], axis=1, keepdims=True)
    res = res_ref[pl.ds(pl.multiple_of(g_ref[0] * 8, 8), 8), :]
    old = jnp.sum(res * res, axis=1, keepdims=True)
    lane = lax.broadcasted_iota(jnp.int32, (8, 128), 1)
    extra = jnp.where(lane == 0, curve, old)
    for r in range(out_ref.shape[0]):
        out_ref[r, :, :256] = jnp.dot(
            half, f_ref[:, r * 256 : (r + 1) * 256], preferred_element_type=f32
        )
        out_ref[r, :, 256:] = extra


def step_body(g_ref, x_ref, res_ref, keep_ref, out_ref):
    image = sum_blocks(x_ref, (0, 256))
    extra = sum_blocks(x_ref, (256, 384))
    curve, old = extra[:, 0:1], extra[:, 1:2]
    alpha = old / curve
    res = res_ref[pl.ds(pl.multiple_of(g_ref[0] * 8, 8), 8), :]
    new = res - alpha * image
    keep_ref[:, :256] = new
    lane = lax.broadcasted_iota(jnp.int32, (8, 128), 1)
    keep_ref[:, 256:] = jnp.where(lane == 0, alpha, old)
    part = jnp.broadcast_to(jnp.sum(new * new, axis=1, keepdims=True), (8, 128))
    for r in range(out_ref.shape[0]):
        out_ref[r] = part


def beta_body(x_ref, keep_ref, out_ref):
    total = sum_blocks(x_ref)
    new, extra = keep_ref[:, :256], keep_ref[:, 256:]
    lane = lax.broadcasted_iota(jnp.int32, (8, 128), 1)
    beta = total[:, 0:1] / extra[:, 1:2]
    extra = jnp.where(lane == 0, extra, beta)
    for r in range(out_ref.shape[0]):
        out_ref[r, :, :256] = new
        out_ref[r, :, 256:] = extra


def final_body(x_ref, it_ref, d_ref, ni_ref, nr_ref, nd_ref):
    for g in range(x_ref.shape[0]):
        rows = slice(g * 8, g * 8 + 8)
        new = x_ref[g, :, :256]
        alpha = x_ref[g, :, 256:257]
        beta = x_ref[g, :, 257:258]
        d = d_ref[rows, :]
        ni_ref[rows, :] = it_ref[rows, :] + alpha * d
        nr_ref[rows, :] = new
        nd_ref[rows, :] = new + beta * d


def local(points, centers, inner_factor, outer_factor, iterate, residual, direction):
    g = (lax.axis_index("zh") * 4 + lax.axis_index("y")).reshape(1)
    c = lax.axis_index("c").reshape(1)
    count = float(points.shape[0] * 256)
    x = call(prep_body, sds((32, 16, 256), bf16), (g, direction), [SM, VM], name="prep")
    x = exchange(x, ROW)
    term, full, x = call(
        inner_body,
        (sds((8, 256), f32), sds((8, 256), f32), sds((32, 8, 256), bf16)),
        (x, inner_factor),
        name="inner",
    )
    x = exchange(x, ROW)
    x = call(outer_body, sds((128, 8, 256), bf16), (x, outer_factor), name="outer")
    x = exchange(x, CHIPS)
    x = x.reshape(8, 16, 8, 256)
    own, other = call(
        kernel_body,
        (sds((8, 16, 8, 256), f32), sds((8, 16, 8, 256), f32)),
        (c, points, centers, x, lax.ppermute(x, "c", SWAP)),
        [SM] + [VM] * 4,
        scratch=[
            pltpu.VMEM((16, points.shape[0], 512), bf16),
            pltpu.VMEM((points.shape[0], 256), bf16),
            pltpu.VMEM((2, 512, 256), bf16),
            pltpu.VMEM((points.shape[0], 64), f32),
            pltpu.VMEM((points.shape[0], 512), bf16),
            pltpu.VMEM((points.shape[0], 512), bf16),
        ],
        vmem=48,
        name="kernel",
    )
    other = lax.ppermute(other, "c", SWAP)
    x = call(add_body, sds((8, 16, 8, 256), bf16), (own, other), name="add")
    x = exchange(x.reshape(128, 8, 256), CHIPS)
    x = call(back_outer_body, sds((32, 8, 256), f32), (x, outer_factor), name="back_outer")
    x = exchange(x, ROW)
    x = call(
        functools.partial(back_inner_body, count),
        sds((32, 8, 384), f32),
        (g, x, inner_factor, term, full, residual),
        [SM] + [VM] * 5,
        name="back_inner",
    )
    x = exchange(x, ROW)
    keep, x = call(
        step_body,
        (sds((8, 384), f32), sds((32, 8, 128), f32)),
        (g, x, residual),
        [SM, VM, VM],
        name="step",
    )
    x = exchange(x, ROW)
    x = call(beta_body, sds((8, 8, 384), f32), (x, keep), name="beta")
    x = exchange(x, GRP)
    out = sds((64, 256), f32)
    return call(final_body, (out, out, out), (x, iterate, direction), name="final")


def solution(mesh):
    fine = Mesh(mesh.devices.reshape(2, 4, 4, 4, 2), ("zh", "y", "zl", "x", "c"))
    placed = (
        P(ALL, None),
        P(),
        P(ROW, None),
        P(ROW, None),
        P(None, ROW),
        P(None, ROW),
        P(None, ROW),
    )
    return jax.shard_map(
        local,
        mesh=fine,
        in_specs=placed,
        out_specs=(P(None, ROW),) * 3,
        check_vma=False,
    )
```

```python
import functools
import jax
import jax.numpy as jnp
from jax import lax
from jax.sharding import Mesh, PartitionSpec as P
from jax.experimental import pallas as pl
from jax.experimental.pallas import tpu as pltpu

ridge_weight = 0.5
bf16, f32 = jnp.bfloat16, jnp.float32
ROW = ("zl", "x", "c")
LINE = ("zl", "x")
CHIPS = ("y", "zl", "x")
ALL = ("zh", "y") + ROW
SWAP = [(0, 1), (1, 0)]
LOG2E = 1.4426950408889634
MIB = 1024 * 1024
LAST = (((1,), (1,)), ((), ()))
VM = pl.BlockSpec(memory_space=pltpu.VMEM)
SM = pl.BlockSpec(memory_space=pltpu.SMEM)


def call(body, outs, args, specs=None, scratch=(), vmem=16, name=None):
    return pl.pallas_call(
        body,
        out_shape=outs,
        in_specs=specs or [VM] * len(args),
        out_specs=jax.tree.map(lambda _: VM, outs),
        scratch_shapes=scratch,
        compiler_params=pltpu.CompilerParams(vmem_limit_bytes=vmem * MIB),
        name=name,
    )(*args)


def sds(shape, dtype):
    return jax.ShapeDtypeStruct(shape, dtype)


def exchange(v, axes):
    return lax.all_to_all(v, axes, 0, 0, tiled=True)


def own_rows(at_ref, ref):
    return ref[pl.ds(pl.multiple_of(at_ref[0] * 16, 16), 16), :]


def columns(at_ref, z, which):
    c = at_ref[1]
    return pl.ds(pl.multiple_of((2 * z + (c if which == 0 else 1 - c)) * 256, 256), 256)


def spread(value, ref):
    for r in range(ref.shape[0]):
        ref[r] = value


def fold(value):
    return jnp.concatenate([value[:8], value[8:]], axis=1)


def unfold(value):
    return jnp.concatenate([value[:, :256], value[:, 256:512]], axis=0)


def prep_body(at_ref, d_ref, out_ref):
    d = own_rows(at_ref, d_ref)
    hi = d.astype(bf16)
    lo = (d - hi.astype(f32)).astype(bf16)
    spread(jnp.concatenate([hi, lo], axis=0), out_ref)


def rows_dot(at_ref, x_ref, y_ref, f_ref):
    acc = None
    for which, ref in ((0, x_ref), (1, y_ref)):
        for z in range(ref.shape[0]):
            part = lax.dot_general(
                ref[z], f_ref[:, columns(at_ref, z, which)], LAST, preferred_element_type=f32
            )
            acc = part if acc is None else acc + part
    return acc


def inner_body(at_ref, x_ref, y_ref, f_ref, term_ref, full_ref, out_ref):
    acc = rows_dot(at_ref, x_ref, y_ref, f_ref)
    term_ref[...] = acc[:16]
    full_ref[...] = acc[:16] + acc[16:]
    spread(acc[:16].astype(bf16), out_ref)


def outer_body(at_ref, x_ref, y_ref, f_ref, out_ref):
    spread(rows_dot(at_ref, x_ref, y_ref, f_ref).astype(bf16), out_ref)


def norm_lanes(rows, first):
    wide = rows.astype(f32)
    lane = lax.broadcasted_iota(jnp.int32, (1, 128), 1)
    norm = jnp.sum(wide * wide, axis=1, keepdims=True) * -0.5
    one = norm.astype(bf16).astype(f32)
    rest = norm - one
    two = rest.astype(bf16).astype(f32)
    three = rest - two
    a, b = (0, 3) if first else (3, 0)
    ones = jnp.where((lane >= b) & (lane < b + 3), 1.0, 0.0)
    out = jnp.where(lane == a + 2, three, ones)
    out = jnp.where(lane == a + 1, two, out)
    return jnp.where(lane == a, one, out).astype(bf16)


def kernel_body(
    at_ref, p_ref, cen_ref, wo_ref, wx_ref, own_ref, oth_ref,
    k_ref, pa_ref, ca_ref, fit_ref, even_ref, odd_ref,
):
    nz = k_ref.shape[0]
    step = 256
    parts = p_ref.shape[0] // step
    c = at_ref[1]
    fit_ref[...] = jnp.zeros_like(fit_ref)
    pa_ref[:, :128] = p_ref[...]
    for i in range(parts):
        rows = pl.ds(i * step, step)
        pa_ref[rows, 128:] = norm_lanes(p_ref[rows, :], True)

    def load(z, slot):
        for h in range(2):
            start = pl.multiple_of((z * 2 + (c if h == 0 else 1 - c)) * 256, 256)
            block = cen_ref[pl.ds(start, 256), :]
            ca_ref[slot, h * 256 : h * 256 + 256, :128] = block
            ca_ref[slot, h * 256 : h * 256 + 256, 128:] = norm_lanes(block, False)

    def fill(z, slot, buf, i):
        rows = pl.ds(i * step, step)
        for h in range(2):
            cols = slice(h * 256, h * 256 + 256)
            d = lax.dot_general(
                pa_ref[rows, :], ca_ref[slot, cols, :], LAST, preferred_element_type=f32
            )
            k = jnp.exp2(d * (LOG2E * 8.0 / 128.0)).astype(bf16)
            k_ref[z, rows, cols] = k
            buf[rows, cols] = k

    def weights(z):
        own = wo_ref[:, z, :, :].reshape(64, 256)
        return jnp.concatenate([own, wx_ref[:, z, :, :].reshape(64, 256)], axis=1)

    def fit(w, buf, i):
        rows = pl.ds(i * step, step)
        fit_ref[rows, :] += lax.dot_general(buf[rows, :], w, LAST, preferred_element_type=f32)

    load(0, 0)
    load(1, 1)
    for i in range(parts):
        fill(0, 0, even_ref, i)

    def pair(h, carry):
        z = 2 * h + 1
        w = weights(z - 1)
        for i in range(parts):
            fit(w, even_ref, i)
            fill(z, 1, odd_ref, i)
        load(z + 1, 0)
        w = weights(z)
        for i in range(parts):
            fit(w, odd_ref, i)
            fill(z + 1, 0, even_ref, i)
        load(z + 2, 1)
        return carry

    lax.fori_loop(0, nz // 2 - 1, pair, 0)
    w = weights(nz - 2)
    for i in range(parts):
        fit(w, even_ref, i)
        fill(nz - 1, 1, odd_ref, i)
    w = weights(nz - 1)
    for i in range(parts):
        fit(w, odd_ref, i)
    fitted = fit_ref[...].T.astype(bf16)

    def second(z, carry):
        for h, ref in ((0, own_ref), (1, oth_ref)):
            n = jnp.dot(fitted, k_ref[z, :, h * 256 : h * 256 + 256], preferred_element_type=f32)
            ref[:, z, :, :] = n.reshape(4, 16, 256).astype(ref.dtype)
        return carry

    lax.fori_loop(0, nz, second, 0, unroll=2)


def add_body(a_ref, b_ref, out_ref):
    out_ref[...] = (a_ref[...] + b_ref[...].astype(f32)).astype(out_ref.dtype)


def sum_blocks(ref):
    parts = [ref[r].astype(f32) for r in range(ref.shape[0])]
    while len(parts) > 1:
        parts = [a + b for a, b in zip(parts[::2], parts[1::2])]
    return parts[0]


def total_body(x_ref, out_ref):
    out_ref[...] = sum_blocks(x_ref)


def back_outer_body(at_ref, x_ref, y_ref, f_ref, own_ref, oth_ref):
    half = (x_ref[...] + y_ref[...]).astype(bf16)
    for which, ref in ((0, own_ref), (1, oth_ref)):
        for z in range(ref.shape[0]):
            ref[z] = jnp.dot(half, f_ref[:, columns(at_ref, z, which)], preferred_element_type=f32)


def back_inner_body(count, at_ref, x_ref, f_ref, term_ref, full_ref, res_ref, own_ref, oth_ref):
    shaped = sum_blocks(x_ref) / count + ridge_weight * term_ref[...]
    half = shaped.astype(bf16)
    curve = jnp.sum(half.astype(f32) * full_ref[...], axis=1, keepdims=True)
    res = own_rows(at_ref, res_ref)
    old = jnp.sum(res * res, axis=1, keepdims=True)
    extra = lanes4(curve, old)
    for which, ref in ((0, own_ref), (1, oth_ref)):
        for z in range(ref.shape[0]):
            ref[z, :, :512] = fold(
                jnp.dot(half, f_ref[:, columns(at_ref, z, which)], preferred_element_type=f32)
            )
            ref[z, :, 512:] = extra


def lanes4(a, b):
    lane = lax.broadcasted_iota(jnp.int32, (1, 128), 1)
    out = jnp.where(lane == 2, b[:8], b[8:])
    out = jnp.where(lane == 1, a[8:], out)
    return jnp.where(lane == 0, a[:8], out)


def pair(tile, at):
    return jnp.concatenate([tile[:, at : at + 1], tile[:, at + 1 : at + 2]], axis=0)


def step_body(at_ref, x_ref, res_ref, keep_ref, out_ref):
    block = sum_blocks(x_ref)
    image, extra = unfold(block), block[:, 512:]
    curve, old = pair(extra, 0), pair(extra, 2)
    alpha = old / curve
    new = own_rows(at_ref, res_ref) - alpha * image
    keep_ref[:, :512] = fold(new)
    keep_ref[:, 512:] = lanes4(alpha, old)
    part = jnp.sum(new * new, axis=1, keepdims=True)
    spread(lanes4(part, part), out_ref)


def beta_body(x_ref, keep_ref, out_ref):
    total = pair(sum_blocks(x_ref), 0)
    extra = keep_ref[:, 512:]
    alpha, old = pair(extra, 0), pair(extra, 2)
    extra = lanes4(alpha, total / old)
    for r in range(out_ref.shape[0]):
        out_ref[r, :, :512] = keep_ref[:, :512]
        out_ref[r, :, 512:] = extra


def final_body(x_ref, it_ref, d_ref, ni_ref, nr_ref, nd_ref):
    for g in range(x_ref.shape[0]):
        rows = slice(g * 16, g * 16 + 16)
        block = x_ref[g]
        new, extra = unfold(block), block[:, 512:]
        d = d_ref[rows, :]
        ni_ref[rows, :] = it_ref[rows, :] + pair(extra, 0) * d
        nr_ref[rows, :] = new
        nd_ref[rows, :] = new + pair(extra, 2) * d


def local(points, centers, inner_factor, outer_factor, iterate, residual, direction):
    at = jnp.stack([lax.axis_index("y"), lax.axis_index("c")])
    count = float(points.shape[0] * 256)

    def swap(v):
        return lax.ppermute(v, "c", SWAP)

    x = call(prep_body, sds((16, 32, 256), bf16), (at, direction), [SM, VM], name="prep")
    x = exchange(x, LINE)
    term, full, x = call(
        inner_body,
        (sds((16, 256), f32), sds((16, 256), f32), sds((16, 16, 256), bf16)),
        (at, x, swap(x), inner_factor),
        [SM] + [VM] * 3,
        name="inner",
    )
    x = exchange(x, LINE)
    x = call(
        outer_body,
        sds((64, 16, 256), bf16),
        (at, x, swap(x), outer_factor),
        [SM] + [VM] * 3,
        name="outer",
    )
    x = exchange(x, CHIPS).reshape(4, 16, 16, 256)
    own, other = call(
        kernel_body,
        (sds((4, 16, 16, 256), f32), sds((4, 16, 16, 256), f32)),
        (at, points, centers, x, swap(x)),
        [SM] + [VM] * 4,
        scratch=[
            pltpu.VMEM((16, points.shape[0], 512), bf16),
            pltpu.VMEM((points.shape[0], 256), bf16),
            pltpu.VMEM((2, 512, 256), bf16),
            pltpu.VMEM((points.shape[0], 64), f32),
            pltpu.VMEM((points.shape[0], 512), bf16),
            pltpu.VMEM((points.shape[0], 512), bf16),
        ],
        vmem=48,
        name="kernel",
    )
    x = call(add_body, sds((4, 16, 16, 256), bf16), (own, swap(other)), name="add")
    x = exchange(x.reshape(64, 16, 256), CHIPS)
    x = call(total_body, sds((16, 256), f32), (x,), name="total")
    own, other = call(
        back_outer_body,
        (sds((16, 16, 256), f32), sds((16, 16, 256), f32)),
        (at, x, lax.ppermute(x, "zh", SWAP), outer_factor),
        [SM] + [VM] * 3,
        name="back_outer",
    )
    x = call(add_body, sds((16, 16, 256), f32), (own, swap(other)), name="add")
    x = exchange(x, LINE)
    own, other = call(
        functools.partial(back_inner_body, count),
        (sds((16, 8, 640), f32), sds((16, 8, 640), f32)),
        (at, x, inner_factor, term, full, residual),
        [SM] + [VM] * 5,
        name="back_inner",
    )
    x = call(add_body, sds((16, 8, 640), f32), (own, swap(other)), name="add")
    x = exchange(x, LINE)
    keep, x = call(
        step_body,
        (sds((8, 640), f32), sds((32, 8, 128), f32)),
        (at, x, residual),
        [SM, VM, VM],
        name="step",
    )
    x = exchange(x, ROW)
    x = call(beta_body, sds((4, 8, 640), f32), (x, keep), name="beta")
    x = exchange(x, ("y",))
    out = sds((64, 256), f32)
    return call(final_body, (out, out, out), (x, iterate, direction), name="final")


def solution(mesh):
    fine = Mesh(mesh.devices.reshape(2, 4, 4, 4, 2), ("zh", "y", "zl", "x", "c"))
    placed = (
        P(ALL, None),
        P(),
        P(ROW, None),
        P(ROW, None),
        P(None, ROW),
        P(None, ROW),
        P(None, ROW),
    )
    return jax.shard_map(
        local,
        mesh=fine,
        in_specs=placed,
        out_specs=(P(None, ROW),) * 3,
        check_vma=False,
    )
```

```python
import functools
import jax
import jax.numpy as jnp
from jax import lax
from jax.sharding import Mesh, PartitionSpec as P
from jax.experimental import pallas as pl
from jax.experimental.pallas import tpu as pltpu

ridge_weight = 0.5
bf16, f32 = jnp.bfloat16, jnp.float32
ROW = ("zl", "x", "c")
LINE = ("zl", "x")
SIDE = ("y", "zl")
FACE = ("zh", "y", "zl")
HALVES = ("zh", "zl", "x", "c")
ALL = ("zh", "y") + ROW
SWAP = [(0, 1), (1, 0)]
LOG2E = 1.4426950408889634
MIB = 1024 * 1024
FILL = 4_000_000_000
LAST = (((1,), (1,)), ((), ()))
VM = pl.BlockSpec(memory_space=pltpu.VMEM)
SM = pl.BlockSpec(memory_space=pltpu.SMEM)


def call(body, outs, args, specs=None, scratch=(), vmem=10, name=None, flops=0):
    return pl.pallas_call(
        body,
        out_shape=outs,
        in_specs=specs or [VM] * len(args),
        out_specs=jax.tree.map(lambda _: VM, outs),
        scratch_shapes=scratch,
        compiler_params=pltpu.CompilerParams(vmem_limit_bytes=vmem * MIB),
        cost_estimate=pl.CostEstimate(flops=flops, bytes_accessed=0, transcendentals=0),
        name=name,
    )(*args)


def sds(shape, dtype):
    return jax.ShapeDtypeStruct(shape, dtype)


def exchange(v, axes):
    return lax.all_to_all(v, axes, 0, 0, tiled=True)


def own_rows(at_ref, ref):
    return ref[pl.ds(pl.multiple_of(at_ref[0] * 16, 16), 16), :]


def eight_rows(at_ref, ref):
    start = at_ref[0] * 16 + at_ref[3] * 8
    return ref[pl.ds(pl.multiple_of(start, 8), 8), :]


def columns(at_ref, z, which):
    c = at_ref[1]
    return pl.ds(pl.multiple_of((2 * z + (c if which == 0 else 1 - c)) * 256, 256), 256)


def spread(value, ref):
    for r in range(ref.shape[0]):
        ref[r] = value


def prep_body(at_ref, d_ref, out_ref):
    d = own_rows(at_ref, d_ref)
    hi = d.astype(bf16)
    lo = (d - hi.astype(f32)).astype(bf16)
    spread(jnp.concatenate([hi, lo], axis=0), out_ref)


def rows_dot(at_ref, x_ref, y_ref, f_ref):
    acc = None
    for which, ref in ((0, x_ref), (1, y_ref)):
        for z in range(ref.shape[0]):
            part = lax.dot_general(
                ref[z], f_ref[:, columns(at_ref, z, which)], LAST, preferred_element_type=f32
            )
            acc = part if acc is None else acc + part
    return acc


def inner_body(at_ref, x_ref, y_ref, f_ref, term_ref, full_ref, out_ref):
    acc = rows_dot(at_ref, x_ref, y_ref, f_ref)
    term_ref[...] = acc[:16]
    full_ref[...] = acc[:16] + acc[16:]
    spread(acc[:16].astype(bf16), out_ref)


def outer_body(at_ref, x_ref, y_ref, f_ref, out_ref):
    spread(rows_dot(at_ref, x_ref, y_ref, f_ref).astype(bf16), out_ref)


def norm_lanes(rows, first):
    wide = rows.astype(f32)
    lane = lax.broadcasted_iota(jnp.int32, (1, 128), 1)
    norm = jnp.sum(wide * wide, axis=1, keepdims=True) * -0.5
    one = norm.astype(bf16).astype(f32)
    rest = norm - one
    two = rest.astype(bf16).astype(f32)
    three = rest - two
    a, b = (0, 3) if first else (3, 0)
    ones = jnp.where((lane >= b) & (lane < b + 3), 1.0, 0.0)
    out = jnp.where(lane == a + 2, three, ones)
    out = jnp.where(lane == a + 1, two, out)
    return jnp.where(lane == a, one, out).astype(bf16)


def fill(at_ref, shift, i, pa_ref, cen_ref, ca_ref, k_ref, fit=None):
    z = i * 4 + (at_ref[2] + shift) % 4
    step = 256
    for h in range(2):
        cols = slice(h * 256, h * 256 + 256)
        block = cen_ref[columns(at_ref, z, h), :]
        ca_ref[cols, :128] = block
        ca_ref[cols, 128:] = norm_lanes(block, False)
    for r in range(pa_ref.shape[0] // step):
        rows = pl.ds(r * step, step)
        if fit is not None:
            fit(i, rows)
        for h in range(2):
            cols = slice(h * 256, h * 256 + 256)
            d = lax.dot_general(pa_ref[rows, :], ca_ref[cols, :], LAST, preferred_element_type=f32)
            k_ref[i, rows, cols] = jnp.exp2(d * (LOG2E * 8.0 / 128.0)).astype(bf16)


def fill_body(at_ref, p_ref, cen_ref, pa_ref, k_ref, ca_ref):
    pa_ref[:, :128] = p_ref[...]
    for r in range(p_ref.shape[0] // 256):
        rows = pl.ds(r * 256, 256)
        pa_ref[rows, 128:] = norm_lanes(p_ref[rows, :], True)

    def chunk(i, carry):
        fill(at_ref, 0, i, pa_ref, cen_ref, ca_ref, k_ref)
        return carry

    lax.fori_loop(0, k_ref.shape[0], chunk, 0)


def fitter(v_ref, u_ref, k_ref, sum_ref):
    def fit(i, rows):
        w = jnp.concatenate(
            [v_ref[:, i, :, :].reshape(64, 256), u_ref[:, i, :, :].reshape(64, 256)], axis=1
        )
        sum_ref[rows, :] += lax.dot_general(
            k_ref[i, rows, :], w, LAST, preferred_element_type=f32
        )

    return fit


def both_body(shift, at_ref, pa_ref, cen_ref, v_ref, u_ref, k_ref, old_ref, next_ref, sum_ref, ca_ref):
    sum_ref[...] = old_ref[...]
    fit = fitter(v_ref, u_ref, k_ref, sum_ref)

    def chunk(i, carry):
        fill(at_ref, shift + 1, i, pa_ref, cen_ref, ca_ref, next_ref, fit)
        return carry

    lax.fori_loop(0, k_ref.shape[0], chunk, 0)


def both_first_body(at_ref, pa_ref, cen_ref, v_ref, u_ref, k_ref, next_ref, sum_ref, ca_ref):
    sum_ref[...] = jnp.zeros_like(sum_ref)
    fit = fitter(v_ref, u_ref, k_ref, sum_ref)

    def chunk(i, carry):
        fill(at_ref, 1, i, pa_ref, cen_ref, ca_ref, next_ref, fit)
        return carry

    lax.fori_loop(0, k_ref.shape[0], chunk, 0)


def fit_body(v_ref, u_ref, k_ref, old_ref, out_ref, sum_ref):
    sum_ref[...] = old_ref[...]
    fit = fitter(v_ref, u_ref, k_ref, sum_ref)

    def chunk(i, carry):
        for r in range(8):
            fit(i, pl.ds(r * 256, 256))
        return carry

    lax.fori_loop(0, k_ref.shape[0], chunk, 0)
    out_ref[...] = sum_ref[...].T.astype(bf16)


def normal_body(fit_ref, k_ref, own_ref, oth_ref):
    fitted = fit_ref[...]

    def chunk(i, carry):
        for h, ref in ((0, own_ref), (1, oth_ref)):
            n = jnp.dot(fitted, k_ref[i, :, h * 256 : h * 256 + 256], preferred_element_type=f32)
            n = n.reshape(4, 2, 8, 256)
            ref[0, :, i, :, :] = n[:, 0]
            ref[1, :, i, :, :] = n[:, 1]
        return carry

    lax.fori_loop(0, k_ref.shape[0], chunk, 0, unroll=2)


def add_body(a_ref, b_ref, out_ref):
    out_ref[...] = (a_ref[...] + b_ref[...].astype(f32)).astype(out_ref.dtype)


def sum_blocks(ref):
    parts = [ref[r].astype(f32) for r in range(ref.shape[0])]
    while len(parts) > 1:
        parts = [a + b for a, b in zip(parts[::2], parts[1::2])]
    return parts[0]


def gather_body(a_ref, b_ref, c_ref, d_ref, e_ref, out_ref):
    out_ref[...] = (
        (a_ref[...] + b_ref[...])
        + (c_ref[...].astype(f32) + d_ref[...].astype(f32))
        + e_ref[...].astype(f32)
    )


def back_outer_body(at_ref, x_ref, f_ref, own_ref, oth_ref):
    half = sum_blocks(x_ref).astype(bf16)
    for which, ref in ((0, own_ref), (1, oth_ref)):
        for z in range(ref.shape[0]):
            ref[z] = jnp.dot(half, f_ref[:, columns(at_ref, z, which)], preferred_element_type=f32)


def back_inner_body(count, at_ref, x_ref, f_ref, term_ref, full_ref, res_ref, own_ref, oth_ref):
    mine = pl.ds(pl.multiple_of(at_ref[3] * 8, 8), 8)
    shaped = sum_blocks(x_ref) / count + ridge_weight * term_ref[mine, :]
    half = shaped.astype(bf16)
    curve = jnp.sum(half.astype(f32) * full_ref[mine, :], axis=1, keepdims=True)
    res = eight_rows(at_ref, res_ref)
    old = jnp.sum(res * res, axis=1, keepdims=True)
    lane = lax.broadcasted_iota(jnp.int32, (8, 128), 1)
    extra = jnp.where(lane == 0, curve, old)
    for which, ref in ((0, own_ref), (1, oth_ref)):
        for z in range(ref.shape[0]):
            ref[z, :, :256] = jnp.dot(
                half, f_ref[:, columns(at_ref, z, which)], preferred_element_type=f32
            )
            ref[z, :, 256:] = extra


def diagonal():
    lane = lax.broadcasted_iota(jnp.int32, (8, 128), 1)
    return lane == lax.broadcasted_iota(jnp.int32, (8, 128), 0)


def step_body(at_ref, x_ref, res_ref, keep_ref, out_ref):
    block = sum_blocks(x_ref)
    curve, old = block[:, 256:257], block[:, 257:258]
    alpha = old / curve
    new = eight_rows(at_ref, res_ref) - alpha * block[:, :256]
    lane = lax.broadcasted_iota(jnp.int32, (8, 128), 1)
    keep_ref[:, :256] = new
    keep_ref[:, 256:] = jnp.where(lane == 0, alpha, old)
    part = jnp.sum(new * new, axis=1, keepdims=True)
    row = jnp.sum(jnp.where(diagonal(), part, 0.0), axis=0, keepdims=True)
    out_ref[...] = jnp.broadcast_to(row, out_ref.shape)


def beta_body(at_ref, x_ref, keep_ref, far_ref, out_ref):
    lane = lax.broadcasted_iota(jnp.int32, (8, 128), 1)
    half = x_ref.shape[0] // 2
    for which, ref in ((0, keep_ref), (1, far_ref)):
        zh = at_ref[3] if which == 0 else 1 - at_ref[3]
        rows = x_ref[pl.ds(pl.multiple_of(zh * half, half), half), :]
        row = jnp.sum(rows, axis=0, keepdims=True)
        total = jnp.sum(jnp.where(diagonal(), row, 0.0), axis=1, keepdims=True)
        extra = ref[:, 256:]
        extra = jnp.where(lane == 0, extra, total / extra[:, 1:2])
        for r in range(out_ref.shape[0]):
            out_ref[r, zh, :, :256] = ref[:, :256]
            out_ref[r, zh, :, 256:] = extra


def final_body(x_ref, it_ref, d_ref, ni_ref, nr_ref, nd_ref):
    for g in range(x_ref.shape[0]):
        for h in range(2):
            rows = slice(g * 16 + h * 8, g * 16 + h * 8 + 8)
            new = x_ref[g, h, :, :256]
            d = d_ref[rows, :]
            ni_ref[rows, :] = it_ref[rows, :] + x_ref[g, h, :, 256:257] * d
            nr_ref[rows, :] = new
            nd_ref[rows, :] = new + x_ref[g, h, :, 257:258] * d


def local(points, centers, inner_factor, outer_factor, iterate, residual, direction):
    at = jnp.stack([lax.axis_index(n) for n in ("y", "c", "x", "zh")])
    here = points.shape[0]
    count = float(here * 256)

    def swap(v):
        return lax.ppermute(v, "c", SWAP)

    def fetch(v, k):
        return lax.ppermute(v, "x", [((i + k) % 4, i) for i in range(4)])

    def send(v, k):
        return lax.ppermute(v, "x", [(i, (i + k) % 4) for i in range(4)])

    x = call(prep_body, sds((16, 32, 256), bf16), (at, direction), [SM, VM], name="prep")
    x = exchange(x, LINE)
    term, full, x = call(
        inner_body,
        (sds((16, 256), f32), sds((16, 256), f32), sds((16, 16, 256), bf16)),
        (at, x, swap(x), inner_factor),
        [SM] + [VM] * 3,
        name="inner",
    )
    x = exchange(x, LINE)
    x = call(
        outer_body,
        sds((16, 16, 256), bf16),
        (at, x, swap(x), outer_factor),
        [SM] + [VM] * 3,
        name="outer",
    )
    v = exchange(x, SIDE).reshape(4, 4, 16, 256)
    vs = [v] + [fetch(v, k) for k in (1, 2, 3)]
    us = [swap(v) for v in vs]
    kernel = sds((4, here, 512), bf16)
    sums = sds((here, 64), f32)
    ca = pltpu.VMEM((512, 256), bf16)
    pa, k0 = call(
        fill_body,
        (sds((here, 256), bf16), kernel),
        (at, points, centers),
        [SM, VM, VM],
        scratch=[ca],
        name="fill",
        flops=FILL,
    )
    k1, fit = call(
        both_first_body,
        (kernel, sums),
        (at, pa, centers, vs[0], us[0], k0),
        [SM] + [VM] * 5,
        scratch=[ca],
        name="both0",
        flops=FILL,
    )
    ks = [k0, k1]
    for k in (1, 2):
        more, fit = call(
            functools.partial(both_body, k),
            (kernel, sums),
            (at, pa, centers, vs[k], us[k], ks[k], fit),
            [SM] + [VM] * 6,
            scratch=[ca],
            name=f"both{k}",
            flops=FILL,
        )
        ks.append(more)
    fitted = call(
        fit_body,
        sds((64, here), bf16),
        (vs[3], us[3], ks[3], fit),
        scratch=[pltpu.VMEM((here, 64), f32)],
        name="fit",
        flops=FILL // 2,
    )
    block = sds((2, 4, 4, 8, 256), f32)
    got = []
    for k in (2, 1, 3, 0):
        own, other = call(
            normal_body, (block, block), (fitted, ks[k]), name=f"normal{k}", flops=FILL // 2
        )
        other = swap(other)
        if k:
            x = call(add_body, sds(block.shape, bf16), (own, other), name="add")
            got.append(send(x, k))
    x = call(gather_body, block, (own, other, *got), name="gather")
    x = exchange(x.reshape(32, 8, 256), FACE)
    own, other = call(
        back_outer_body,
        (sds((16, 8, 256), f32), sds((16, 8, 256), f32)),
        (at, x, outer_factor),
        [SM] + [VM] * 2,
        name="back_outer",
    )
    x = call(add_body, sds((16, 8, 256), f32), (own, swap(other)), name="add")
    x = exchange(x, LINE)
    own, other = call(
        functools.partial(back_inner_body, count),
        (sds((16, 8, 384), f32), sds((16, 8, 384), f32)),
        (at, x, inner_factor, term, full, residual),
        [SM] + [VM] * 5,
        name="back_inner",
    )
    x = call(add_body, sds((16, 8, 384), f32), (own, swap(other)), name="add")
    x = exchange(x, LINE)
    keep, x = call(
        step_body,
        (sds((8, 384), f32), sds((64, 128), f32)),
        (at, x, residual),
        [SM, VM, VM],
        name="step",
    )
    far = lax.ppermute(keep, "zh", SWAP)
    x = exchange(x, HALVES)
    x = call(
        beta_body, sds((4, 2, 8, 384), f32), (at, x, keep, far), [SM, VM, VM, VM], name="beta"
    )
    x = exchange(x, ("y",))
    out = sds((64, 256), f32)
    return call(final_body, (out, out, out), (x, iterate, direction), name="final")


def solution(mesh):
    fine = Mesh(mesh.devices.reshape(2, 4, 4, 4, 2), ("zh", "y", "zl", "x", "c"))
    placed = (
        P(ALL, None),
        P(),
        P(ROW, None),
        P(ROW, None),
        P(None, ROW),
        P(None, ROW),
        P(None, ROW),
    )
    return jax.shard_map(
        local,
        mesh=fine,
        in_specs=placed,
        out_specs=(P(None, ROW),) * 3,
        check_vma=False,
    )
```

```python
import functools
import jax
import jax.numpy as jnp
from jax import lax
from jax.sharding import Mesh, PartitionSpec as P
from jax.experimental import pallas as pl
from jax.experimental.pallas import tpu as pltpu

ridge_weight = 0.5
bf16, f32 = jnp.bfloat16, jnp.float32
ROW = ("zl", "x", "c")
LINE = ("zl", "x")
SIDE = ("y", "zl")
FACE = ("zh", "y", "zl")
HALVES = ("zh", "zl", "x", "c")
ALL = ("zh", "y") + ROW
SWAP = [(0, 1), (1, 0)]
LOG2E = 1.4426950408889634
MIB = 1024 * 1024
FILL = 4_000_000_000
LAST = (((1,), (1,)), ((), ()))
VM = pl.BlockSpec(memory_space=pltpu.VMEM)
SM = pl.BlockSpec(memory_space=pltpu.SMEM)


def call(body, outs, args, specs=None, scratch=(), vmem=10, flops=0):
    return pl.pallas_call(
        body,
        out_shape=outs,
        in_specs=specs or [VM] * len(args),
        out_specs=jax.tree.map(lambda _: VM, outs),
        scratch_shapes=scratch,
        compiler_params=pltpu.CompilerParams(vmem_limit_bytes=vmem * MIB),
        cost_estimate=pl.CostEstimate(flops=flops, bytes_accessed=0, transcendentals=0),
    )(*args)


def sds(shape, dtype):
    return jax.ShapeDtypeStruct(shape, dtype)


def exchange(v, axes):
    return lax.all_to_all(v, axes, 0, 0, tiled=True)


def own_rows(at_ref, ref):
    return ref[pl.ds(pl.multiple_of(at_ref[0] * 16, 16), 16), :]


def eight_rows(at_ref, ref):
    start = at_ref[0] * 16 + at_ref[3] * 8
    return ref[pl.ds(pl.multiple_of(start, 8), 8), :]


def columns(at_ref, z, which):
    c = at_ref[1]
    return pl.ds(pl.multiple_of((2 * z + (c if which == 0 else 1 - c)) * 256, 256), 256)


def spread(value, ref):
    for r in range(ref.shape[0]):
        ref[r] = value


def prep_body(at_ref, d_ref, out_ref):
    d = own_rows(at_ref, d_ref)
    hi = d.astype(bf16)
    lo = (d - hi.astype(f32)).astype(bf16)
    spread(jnp.concatenate([hi, lo], axis=0), out_ref)


def rows_dot(at_ref, x_ref, y_ref, f_ref):
    acc = None
    for which, ref in ((0, x_ref), (1, y_ref)):
        for z in range(ref.shape[0]):
            part = lax.dot_general(
                ref[z], f_ref[:, columns(at_ref, z, which)], LAST, preferred_element_type=f32
            )
            acc = part if acc is None else acc + part
    return acc


def inner_body(at_ref, x_ref, y_ref, hbm_ref, term_ref, full_ref, out_ref, f_ref, sem):
    parts = sem.shape[0]
    width = hbm_ref.shape[1] // parts
    copies = [
        pltpu.make_async_copy(
            hbm_ref.at[:, pl.ds(q * width, width)], f_ref.at[:, pl.ds(q * width, width)], sem.at[q]
        )
        for q in range(parts)
    ]
    for copy in copies:
        copy.start()
    acc = None
    count = x_ref.shape[0] // parts
    for q in range(parts):
        copies[q].wait()
        for z in range(q * count, q * count + count):
            for which, ref in ((0, x_ref), (1, y_ref)):
                part = lax.dot_general(
                    ref[z], f_ref[:, columns(at_ref, z, which)], LAST, preferred_element_type=f32
                )
                acc = part if acc is None else acc + part
    term_ref[...] = acc[:16]
    full_ref[...] = acc[:16] + acc[16:]
    spread(acc[:16].astype(bf16), out_ref)


def outer_body(at_ref, x_ref, y_ref, f_ref, out_ref):
    spread(rows_dot(at_ref, x_ref, y_ref, f_ref).astype(bf16), out_ref)


def norm_lanes(rows, first):
    wide = rows.astype(f32)
    lane = lax.broadcasted_iota(jnp.int32, (1, 128), 1)
    norm = jnp.sum(wide * wide, axis=1, keepdims=True) * -0.5
    one = norm.astype(bf16).astype(f32)
    rest = norm - one
    two = rest.astype(bf16).astype(f32)
    three = rest - two
    a, b = (0, 3) if first else (3, 0)
    ones = jnp.where((lane >= b) & (lane < b + 3), 1.0, 0.0)
    out = jnp.where(lane == a + 2, three, ones)
    out = jnp.where(lane == a + 1, two, out)
    return jnp.where(lane == a, one, out).astype(bf16)


def chunks(at_ref, shift, pa_ref, cen_ref, ca_ref, k_ref, fit=None):
    step = 256

    def load(i, slot):
        z = i * 4 + (at_ref[2] + shift) % 4
        for h in range(2):
            cols = slice(h * 256, h * 256 + 256)
            block = cen_ref[columns(at_ref, z, h), :]
            ca_ref[slot, cols, :128] = block
            ca_ref[slot, cols, 128:] = norm_lanes(block, False)

    load(0, 0)

    def two(j, carry):
        for slot in range(2):
            i = j * 2 + slot
            load(jnp.minimum(i + 1, 3), 1 - slot)
            w = None if fit is None else fit.weights(i)
            for r in range(pa_ref.shape[0] // step):
                rows = pl.ds(r * step, step)
                if fit is not None:
                    fit.add(w, i, rows)
                for h in range(2):
                    cols = slice(h * 256, h * 256 + 256)
                    d = lax.dot_general(
                        pa_ref[rows, :], ca_ref[slot, cols, :], LAST, preferred_element_type=f32
                    )
                    k_ref[i, rows, cols] = jnp.exp2(d * (LOG2E * 8.0 / 128.0)).astype(bf16)
        return carry

    lax.fori_loop(0, 2, two, 0)


def fill_body(at_ref, p_ref, cen_ref, pa_ref, k_ref, ca_ref):
    pa_ref[:, :128] = p_ref[...]
    for r in range(p_ref.shape[0] // 256):
        rows = pl.ds(r * 256, 256)
        pa_ref[rows, 128:] = norm_lanes(p_ref[rows, :], True)
    chunks(at_ref, 0, pa_ref, cen_ref, ca_ref, k_ref)


class Fitter:
    def __init__(self, v_ref, u_ref, k_ref, sum_ref):
        self.refs = v_ref, u_ref, k_ref, sum_ref

    def weights(self, i):
        v_ref, u_ref = self.refs[:2]
        return jnp.concatenate(
            [v_ref[:, i, :, :].reshape(64, 256), u_ref[:, i, :, :].reshape(64, 256)], axis=1
        )

    def add(self, w, i, rows):
        k_ref, sum_ref = self.refs[2:]
        sum_ref[rows, :] += lax.dot_general(
            k_ref[i, rows, :], w, LAST, preferred_element_type=f32
        )


def both_body(shift, at_ref, pa_ref, cen_ref, v_ref, u_ref, k_ref, old_ref, next_ref, sum_ref, ca_ref):
    sum_ref[...] = old_ref[...]
    fit = Fitter(v_ref, u_ref, k_ref, sum_ref)
    chunks(at_ref, shift + 1, pa_ref, cen_ref, ca_ref, next_ref, fit)


def both_first_body(at_ref, pa_ref, cen_ref, v_ref, u_ref, k_ref, next_ref, sum_ref, ca_ref):
    sum_ref[...] = jnp.zeros_like(sum_ref)
    fit = Fitter(v_ref, u_ref, k_ref, sum_ref)
    chunks(at_ref, 1, pa_ref, cen_ref, ca_ref, next_ref, fit)


def fit_body(v_ref, u_ref, k_ref, old_ref, out_ref, sum_ref):
    sum_ref[...] = old_ref[...]
    fit = Fitter(v_ref, u_ref, k_ref, sum_ref)

    def chunk(i, carry):
        w = fit.weights(i)
        for r in range(k_ref.shape[1] // 256):
            fit.add(w, i, pl.ds(r * 256, 256))
        return carry

    lax.fori_loop(0, k_ref.shape[0], chunk, 0)
    out_ref[...] = sum_ref[...].T.astype(bf16)


def normal_body(fit_ref, k_ref, own_ref, oth_ref):
    fitted = fit_ref[...]

    def chunk(i, carry):
        for h, ref in ((0, own_ref), (1, oth_ref)):
            n = jnp.dot(fitted, k_ref[i, :, h * 256 : h * 256 + 256], preferred_element_type=f32)
            n = n.reshape(4, 2, 8, 256)
            ref[0, :, i, :, :] = n[:, 0]
            ref[1, :, i, :, :] = n[:, 1]
        return carry

    lax.fori_loop(0, k_ref.shape[0], chunk, 0, unroll=2)


def add_body(a_ref, b_ref, out_ref):
    out_ref[...] = (a_ref[...] + b_ref[...].astype(f32)).astype(out_ref.dtype)


def sum_blocks(ref):
    parts = [ref[r].astype(f32) for r in range(ref.shape[0])]
    while len(parts) > 1:
        parts = [a + b for a, b in zip(parts[::2], parts[1::2])]
    return parts[0]


def gather_body(a_ref, b_ref, c_ref, d_ref, e_ref, out_ref):
    total = (
        (a_ref[...] + b_ref[...])
        + (c_ref[...].astype(f32) + d_ref[...].astype(f32))
        + e_ref[...].astype(f32)
    )
    out_ref[...] = total.astype(out_ref.dtype)


def back_outer_body(at_ref, x_ref, f_ref, own_ref, oth_ref):
    half = sum_blocks(x_ref).astype(bf16)
    for which, ref in ((0, own_ref), (1, oth_ref)):
        for z in range(ref.shape[0]):
            ref[z] = jnp.dot(half, f_ref[:, columns(at_ref, z, which)], preferred_element_type=f32)


def back_inner_body(count, at_ref, x_ref, f_ref, term_ref, full_ref, res_ref, own_ref, oth_ref):
    mine = pl.ds(pl.multiple_of(at_ref[3] * 8, 8), 8)
    shaped = sum_blocks(x_ref) / count + ridge_weight * term_ref[mine, :]
    half = shaped.astype(bf16)
    curve = jnp.sum(half.astype(f32) * full_ref[mine, :], axis=1, keepdims=True)
    res = eight_rows(at_ref, res_ref)
    old = jnp.sum(res * res, axis=1, keepdims=True)
    lane = lax.broadcasted_iota(jnp.int32, (8, 128), 1)
    extra = jnp.where(lane == 0, curve, old)
    for which, ref in ((0, own_ref), (1, oth_ref)):
        for z in range(ref.shape[0]):
            ref[z, :, :256] = jnp.dot(
                half, f_ref[:, columns(at_ref, z, which)], preferred_element_type=f32
            )
            ref[z, :, 256:] = extra


def diagonal():
    lane = lax.broadcasted_iota(jnp.int32, (8, 128), 1)
    return lane == lax.broadcasted_iota(jnp.int32, (8, 128), 0)


def step_body(at_ref, x_ref, res_ref, keep_ref, out_ref):
    block = sum_blocks(x_ref)
    curve, old = block[:, 256:257], block[:, 257:258]
    alpha = old / curve
    new = eight_rows(at_ref, res_ref) - alpha * block[:, :256]
    lane = lax.broadcasted_iota(jnp.int32, (8, 128), 1)
    keep_ref[:, :256] = new
    keep_ref[:, 256:] = jnp.where(lane == 0, alpha, old)
    part = jnp.sum(new * new, axis=1, keepdims=True)
    row = jnp.sum(jnp.where(diagonal(), part, 0.0), axis=0, keepdims=True)
    out_ref[...] = jnp.broadcast_to(row, out_ref.shape)


def beta_body(at_ref, x_ref, keep_ref, far_ref, out_ref):
    lane = lax.broadcasted_iota(jnp.int32, (8, 128), 1)
    half = x_ref.shape[0] // 2
    for which, ref in ((0, keep_ref), (1, far_ref)):
        zh = at_ref[3] if which == 0 else 1 - at_ref[3]
        rows = x_ref[pl.ds(pl.multiple_of(zh * half, half), half), :]
        row = jnp.sum(rows, axis=0, keepdims=True)
        total = jnp.sum(jnp.where(diagonal(), row, 0.0), axis=1, keepdims=True)
        extra = ref[:, 256:]
        extra = jnp.where(lane == 0, extra, total / extra[:, 1:2])
        for r in range(out_ref.shape[0]):
            out_ref[r, zh, :, :256] = ref[:, :256]
            out_ref[r, zh, :, 256:] = extra


def final_body(x_ref, it_ref, d_ref, ni_ref, nr_ref, nd_ref):
    for g in range(x_ref.shape[0]):
        for h in range(2):
            rows = slice(g * 16 + h * 8, g * 16 + h * 8 + 8)
            new = x_ref[g, h, :, :256]
            d = d_ref[rows, :]
            ni_ref[rows, :] = it_ref[rows, :] + x_ref[g, h, :, 256:257] * d
            nr_ref[rows, :] = new
            nd_ref[rows, :] = new + x_ref[g, h, :, 257:258] * d


def iteration(points, centers, inner_factor, outer_factor, iterate, residual, direction):
    at = jnp.stack([lax.axis_index(n) for n in ("y", "c", "x", "zh")])
    here = points.shape[0]
    count = float(here * 256)

    def swap(v):
        return lax.ppermute(v, "c", SWAP)

    def fetch(v, k):
        return lax.ppermute(v, "x", [((i + k) % 4, i) for i in range(4)])

    def send(v, k):
        return lax.ppermute(v, "x", [(i, (i + k) % 4) for i in range(4)])

    x = call(prep_body, sds((16, 32, 256), bf16), (at, direction), [SM, VM])
    x = exchange(x, LINE)
    term, full, x = call(
        inner_body,
        (sds((16, 256), f32), sds((16, 256), f32), sds((16, 16, 256), bf16)),
        (at, x, swap(x), pltpu.with_memory_space_constraint(inner_factor, pltpu.HBM)),
        [SM, VM, VM, pl.BlockSpec(memory_space=pltpu.HBM)],
        scratch=[pltpu.VMEM(inner_factor.shape, bf16), pltpu.SemaphoreType.DMA((4,))],
    )
    x = exchange(x, LINE)
    x = call(outer_body, sds((16, 16, 256), bf16), (at, x, swap(x), outer_factor), [SM] + [VM] * 3)
    v = exchange(x, SIDE).reshape(4, 4, 16, 256)
    vs = [v] + [fetch(v, k) for k in (1, 2, 3)]
    us = [swap(v) for v in vs]
    kernel = sds((4, here, 512), bf16)
    sums = sds((here, 64), f32)
    ca = pltpu.VMEM((2, 512, 256), bf16)
    pa, k0 = call(
        fill_body,
        (sds((here, 256), bf16), kernel),
        (at, points, centers),
        [SM, VM, VM],
        scratch=[ca],
        flops=FILL,
    )
    k1, fit = call(
        both_first_body,
        (kernel, sums),
        (at, pa, centers, vs[0], us[0], k0),
        [SM] + [VM] * 5,
        scratch=[ca],
        flops=FILL,
    )
    ks = [k0, k1]
    for k in (1, 2):
        more, fit = call(
            functools.partial(both_body, k),
            (kernel, sums),
            (at, pa, centers, vs[k], us[k], ks[k], fit),
            [SM] + [VM] * 6,
            scratch=[ca],
            flops=FILL,
        )
        ks.append(more)
    fitted = call(
        fit_body,
        sds((64, here), bf16),
        (vs[3], us[3], ks[3], fit),
        scratch=[pltpu.VMEM((here, 64), f32)],
        flops=FILL // 2,
    )
    block = sds((2, 4, 4, 8, 256), f32)
    got = []
    for k in (2, 1, 3, 0):
        own, other = call(normal_body, (block, block), (fitted, ks[k]), flops=FILL // 2)
        other = swap(other)
        if k:
            x = call(add_body, sds(block.shape, bf16), (own, other))
            got.append(send(x, k))
    x = call(gather_body, sds(block.shape, bf16), (own, other, *got))
    x = exchange(x.reshape(32, 8, 256), FACE)
    own, other = call(
        back_outer_body,
        (sds((16, 8, 256), f32), sds((16, 8, 256), f32)),
        (at, x, outer_factor),
        [SM] + [VM] * 2,
    )
    x = call(add_body, sds((16, 8, 256), f32), (own, swap(other)))
    x = exchange(x, LINE)
    own, other = call(
        functools.partial(back_inner_body, count),
        (sds((16, 8, 384), f32), sds((16, 8, 384), f32)),
        (at, x, inner_factor, term, full, residual),
        [SM] + [VM] * 5,
    )
    x = call(add_body, sds((16, 8, 384), f32), (own, swap(other)))
    x = exchange(x, LINE)
    keep, x = call(
        step_body, (sds((8, 384), f32), sds((64, 128), f32)), (at, x, residual), [SM, VM, VM]
    )
    far = lax.ppermute(keep, "zh", SWAP)
    x = exchange(x, HALVES)
    x = call(beta_body, sds((4, 2, 8, 384), f32), (at, x, keep, far), [SM, VM, VM, VM])
    x = exchange(x, ("y",))
    out = sds((64, 256), f32)
    return call(final_body, (out, out, out), (x, iterate, direction))


def solution(mesh):
    fine = Mesh(mesh.devices.reshape(2, 4, 4, 4, 2), ("zh", "y", "zl", "x", "c"))
    placed = (
        P(ALL, None),
        P(),
        P(ROW, None),
        P(ROW, None),
        P(None, ROW),
        P(None, ROW),
        P(None, ROW),
    )
    return jax.shard_map(
        iteration,
        mesh=fine,
        in_specs=placed,
        out_specs=(P(None, ROW),) * 3,
        check_vma=False,
    )
```

```python
import functools
import jax
import jax.numpy as jnp
from jax import lax
from jax.sharding import Mesh, PartitionSpec as P
from jax.experimental import pallas as pl
from jax.experimental.pallas import tpu as pltpu

ridge_weight = 0.5
bf16, f32 = jnp.bfloat16, jnp.float32
ROW = ("zl", "x", "c")
LINE = ("zl", "x")
SIDE = ("y", "zl")
FACE = ("zh", "y", "zl")
ALL = ("zh", "y") + ROW
SWAP = [(0, 1), (1, 0)]
LOG2E = 1.4426950408889634
MIB = 1024 * 1024
FILL = 4_000_000_000
LAST = (((1,), (1,)), ((), ()))
VM = pl.BlockSpec(memory_space=pltpu.VMEM)
SM = pl.BlockSpec(memory_space=pltpu.SMEM)


def call(body, outs, args, specs=None, scratch=(), vmem=10, flops=0):
    return pl.pallas_call(
        body,
        out_shape=outs,
        in_specs=specs or [VM] * len(args),
        out_specs=jax.tree.map(lambda _: VM, outs),
        scratch_shapes=scratch,
        compiler_params=pltpu.CompilerParams(vmem_limit_bytes=vmem * MIB),
        cost_estimate=pl.CostEstimate(flops=flops, bytes_accessed=0, transcendentals=0),
    )(*args)


def sds(shape, dtype):
    return jax.ShapeDtypeStruct(shape, dtype)


def exchange(v, axes):
    return lax.all_to_all(v, axes, 0, 0, tiled=True)


def own_rows(at_ref, ref):
    return ref[pl.ds(pl.multiple_of(at_ref[0] * 16, 16), 16), :]


def eight_rows(at_ref, ref):
    start = at_ref[0] * 16 + at_ref[3] * 8
    return ref[pl.ds(pl.multiple_of(start, 8), 8), :]


def columns(at_ref, z, which):
    c = at_ref[1]
    return pl.ds(pl.multiple_of((2 * z + (c if which == 0 else 1 - c)) * 256, 256), 256)


def spread(value, ref):
    for r in range(ref.shape[0]):
        ref[r] = value


def prep_body(at_ref, d_ref, out_ref):
    d = own_rows(at_ref, d_ref)
    hi = d.astype(bf16)
    lo = (d - hi.astype(f32)).astype(bf16)
    spread(jnp.concatenate([hi, lo], axis=0), out_ref)


def rows_dot(at_ref, x_ref, y_ref, f_ref):
    acc = None
    for which, ref in ((0, x_ref), (1, y_ref)):
        for z in range(ref.shape[0]):
            part = lax.dot_general(
                ref[z], f_ref[:, columns(at_ref, z, which)], LAST, preferred_element_type=f32
            )
            acc = part if acc is None else acc + part
    return acc


def inner_body(at_ref, x_ref, y_ref, hbm_ref, term_ref, full_ref, out_ref, f_ref, sem):
    parts = sem.shape[0]
    width = hbm_ref.shape[1] // parts
    copies = [
        pltpu.make_async_copy(
            hbm_ref.at[:, pl.ds(q * width, width)], f_ref.at[:, pl.ds(q * width, width)], sem.at[q]
        )
        for q in range(parts)
    ]
    for copy in copies[:2]:
        copy.start()
    acc = None
    count = x_ref.shape[0] // parts
    for q in range(parts):
        copies[q].wait()
        if q + 2 < parts:
            copies[q + 2].start()
        for z in range(q * count, q * count + count):
            for which, ref in ((0, x_ref), (1, y_ref)):
                part = lax.dot_general(
                    ref[z], f_ref[:, columns(at_ref, z, which)], LAST, preferred_element_type=f32
                )
                acc = part if acc is None else acc + part
    term_ref[...] = acc[:16]
    full_ref[...] = acc[:16] + acc[16:]
    spread(acc[:16].astype(bf16), out_ref)


def outer_body(at_ref, x_ref, y_ref, f_ref, out_ref):
    spread(rows_dot(at_ref, x_ref, y_ref, f_ref).astype(bf16), out_ref)


def norm_lanes(rows, first):
    wide = rows.astype(f32)
    lane = lax.broadcasted_iota(jnp.int32, (1, 128), 1)
    norm = jnp.sum(wide * wide, axis=1, keepdims=True) * -0.5
    one = norm.astype(bf16).astype(f32)
    rest = norm - one
    two = rest.astype(bf16).astype(f32)
    three = rest - two
    a, b = (0, 3) if first else (3, 0)
    ones = jnp.where((lane >= b) & (lane < b + 3), 1.0, 0.0)
    out = jnp.where(lane == a + 2, three, ones)
    out = jnp.where(lane == a + 1, two, out)
    return jnp.where(lane == a, one, out).astype(bf16)


def chunks(at_ref, shift, pa_ref, cen_ref, ca_ref, k_ref, fit=None):
    step = 256

    def load(i, slot):
        z = i * 4 + (at_ref[2] ^ shift)
        for h in range(2):
            cols = slice(h * 256, h * 256 + 256)
            block = cen_ref[columns(at_ref, z, h), :]
            ca_ref[slot, cols, :128] = block
            ca_ref[slot, cols, 128:] = norm_lanes(block, False)

    load(0, 0)

    def two(j, carry):
        for slot in range(2):
            i = j * 2 + slot
            load(jnp.minimum(i + 1, 3), 1 - slot)
            w = None if fit is None else fit.weights(i)
            for r in range(pa_ref.shape[0] // step):
                rows = pl.ds(r * step, step)
                if fit is not None:
                    fit.add(w, i, rows)
                for h in range(2):
                    cols = slice(h * 256, h * 256 + 256)
                    d = lax.dot_general(
                        pa_ref[rows, :], ca_ref[slot, cols, :], LAST, preferred_element_type=f32
                    )
                    k_ref[i, rows, cols] = jnp.exp2(d * (LOG2E * 8.0 / 128.0)).astype(bf16)
        return carry

    lax.fori_loop(0, 2, two, 0)


def fill_body(at_ref, p_ref, cen_ref, pa_ref, k_ref, ca_ref):
    pa_ref[:, :128] = p_ref[...]
    for r in range(p_ref.shape[0] // 256):
        rows = pl.ds(r * 256, 256)
        pa_ref[rows, 128:] = norm_lanes(p_ref[rows, :], True)
    chunks(at_ref, 0, pa_ref, cen_ref, ca_ref, k_ref)


class Fitter:
    def __init__(self, v_ref, u_ref, k_ref, sum_ref):
        self.refs = v_ref, u_ref, k_ref, sum_ref

    def weights(self, i):
        v_ref, u_ref = self.refs[:2]
        return jnp.concatenate(
            [v_ref[:, i, :, :].reshape(64, 256), u_ref[:, i, :, :].reshape(64, 256)], axis=1
        )

    def add(self, w, i, rows):
        k_ref, sum_ref = self.refs[2:]
        sum_ref[rows, :] += lax.dot_general(
            k_ref[i, rows, :], w, LAST, preferred_element_type=f32
        )


def both_body(shift, at_ref, pa_ref, cen_ref, v_ref, u_ref, k_ref, old_ref, next_ref, sum_ref, ca_ref):
    sum_ref[...] = old_ref[...]
    fit = Fitter(v_ref, u_ref, k_ref, sum_ref)
    chunks(at_ref, shift + 1, pa_ref, cen_ref, ca_ref, next_ref, fit)


def both_first_body(at_ref, pa_ref, cen_ref, v_ref, u_ref, k_ref, next_ref, sum_ref, ca_ref):
    sum_ref[...] = jnp.zeros_like(sum_ref)
    fit = Fitter(v_ref, u_ref, k_ref, sum_ref)
    chunks(at_ref, 1, pa_ref, cen_ref, ca_ref, next_ref, fit)


def fit_body(v_ref, u_ref, k_ref, old_ref, out_ref, sum_ref):
    sum_ref[...] = old_ref[...]
    fit = Fitter(v_ref, u_ref, k_ref, sum_ref)

    def chunk(i, carry):
        w = fit.weights(i)
        for r in range(k_ref.shape[1] // 256):
            fit.add(w, i, pl.ds(r * 256, 256))
        return carry

    lax.fori_loop(0, k_ref.shape[0], chunk, 0)
    out_ref[...] = sum_ref[...].T.astype(bf16)


def normal_body(fit_ref, k_ref, own_ref, oth_ref):
    fitted = fit_ref[...]

    def chunk(i, carry):
        for h, ref in ((0, own_ref), (1, oth_ref)):
            n = jnp.dot(fitted, k_ref[i, :, h * 256 : h * 256 + 256], preferred_element_type=f32)
            n = n.reshape(4, 2, 8, 256)
            ref[0, :, i, :, :] = n[:, 0]
            ref[1, :, i, :, :] = n[:, 1]
        return carry

    lax.fori_loop(0, k_ref.shape[0], chunk, 0, unroll=2)


def add_body(a_ref, b_ref, out_ref):
    out_ref[...] = (a_ref[...] + b_ref[...].astype(f32)).astype(out_ref.dtype)


def sum_blocks(ref):
    parts = [ref[r].astype(f32) for r in range(ref.shape[0])]
    while len(parts) > 1:
        parts = [a + b for a, b in zip(parts[::2], parts[1::2])]
    return parts[0]


def gather_body(a_ref, b_ref, c_ref, d_ref, e_ref, out_ref):
    total = (
        (a_ref[...] + b_ref[...])
        + (c_ref[...].astype(f32) + d_ref[...].astype(f32))
        + e_ref[...].astype(f32)
    )
    out_ref[...] = total.astype(out_ref.dtype)


def back_outer_body(at_ref, x_ref, f_ref, own_ref, oth_ref):
    half = sum_blocks(x_ref).astype(bf16)
    for which, ref in ((0, own_ref), (1, oth_ref)):
        for z in range(ref.shape[0]):
            ref[z] = jnp.dot(half, f_ref[:, columns(at_ref, z, which)], preferred_element_type=f32)


def back_inner_body(count, at_ref, x_ref, f_ref, term_ref, full_ref, res_ref, own_ref, oth_ref):
    mine = pl.ds(pl.multiple_of(at_ref[3] * 8, 8), 8)
    shaped = sum_blocks(x_ref) / count + ridge_weight * term_ref[mine, :]
    half = shaped.astype(bf16)
    curve = jnp.sum(half.astype(f32) * full_ref[mine, :], axis=1, keepdims=True)
    res = eight_rows(at_ref, res_ref)
    old = jnp.sum(res * res, axis=1, keepdims=True)
    lane = lax.broadcasted_iota(jnp.int32, (8, 128), 1)
    extra = jnp.where(lane == 0, curve, old)
    for which, ref in ((0, own_ref), (1, oth_ref)):
        for z in range(ref.shape[0]):
            ref[z, :, :256] = jnp.dot(
                half, f_ref[:, columns(at_ref, z, which)], preferred_element_type=f32
            )
            ref[z, :, 256:] = extra


def diagonal():
    lane = lax.broadcasted_iota(jnp.int32, (8, 128), 1)
    return lane == lax.broadcasted_iota(jnp.int32, (8, 128), 0)


def step_body(at_ref, x_ref, res_ref, keep_ref, out_ref):
    block = sum_blocks(x_ref)
    curve, old = block[:, 256:257], block[:, 257:258]
    alpha = old / curve
    new = eight_rows(at_ref, res_ref) - alpha * block[:, :256]
    lane = lax.broadcasted_iota(jnp.int32, (8, 128), 1)
    keep_ref[:, :256] = new
    keep_ref[:, 256:] = jnp.where(lane == 0, alpha, old)
    part = jnp.sum(new * new, axis=1, keepdims=True)
    row = jnp.sum(jnp.where(diagonal(), part, 0.0), axis=0, keepdims=True)
    out_ref[...] = jnp.broadcast_to(row, out_ref.shape)


def beta_body(x_ref, keep_ref, out_ref):
    lane = lax.broadcasted_iota(jnp.int32, (8, 128), 1)
    row = jnp.sum(x_ref[...], axis=0, keepdims=True)
    total = jnp.sum(jnp.where(diagonal(), row, 0.0), axis=1, keepdims=True)
    extra = keep_ref[:, 256:]
    extra = jnp.where(lane == 0, extra, total / extra[:, 1:2])
    for r in range(out_ref.shape[0]):
        out_ref[r, :, :256] = keep_ref[:, :256]
        out_ref[r, :, 256:] = extra


def final_body(x_ref, it_ref, d_ref, ni_ref, nr_ref, nd_ref):
    for g in range(x_ref.shape[0]):
        start = (g % 4) * 16 + (g // 4) * 8
        rows = slice(start, start + 8)
        new = x_ref[g, :, :256]
        d = d_ref[rows, :]
        ni_ref[rows, :] = it_ref[rows, :] + x_ref[g, :, 256:257] * d
        nr_ref[rows, :] = new
        nd_ref[rows, :] = new + x_ref[g, :, 257:258] * d


def iteration(points, centers, inner_factor, outer_factor, iterate, residual, direction):
    at = jnp.stack([lax.axis_index(n) for n in ("y", "c", "x", "zh")])
    here = points.shape[0]
    count = float(here * 256)

    def swap(v):
        return lax.ppermute(v, "c", SWAP)

    def across(v, k):
        return lax.ppermute(v, "x", [(i, i ^ k) for i in range(4)])

    x = call(prep_body, sds((16, 32, 256), bf16), (at, direction), [SM, VM])
    x = exchange(x, LINE)
    term, full, x = call(
        inner_body,
        (sds((16, 256), f32), sds((16, 256), f32), sds((16, 16, 256), bf16)),
        (at, x, swap(x), pltpu.with_memory_space_constraint(inner_factor, pltpu.HBM)),
        [SM, VM, VM, pl.BlockSpec(memory_space=pltpu.HBM)],
        scratch=[pltpu.VMEM(inner_factor.shape, bf16), pltpu.SemaphoreType.DMA((8,))],
    )
    x = exchange(x, LINE)
    x = call(outer_body, sds((16, 16, 256), bf16), (at, x, swap(x), outer_factor), [SM] + [VM] * 3)
    v = exchange(x, SIDE).reshape(4, 4, 16, 256)
    vs = [v] + [across(v, k) for k in (1, 2, 3)]
    us = [swap(v) for v in vs]
    kernel = sds((4, here, 512), bf16)
    sums = sds((here, 64), f32)
    ca = pltpu.VMEM((2, 512, 256), bf16)
    pa, k0 = call(
        fill_body,
        (sds((here, 256), bf16), kernel),
        (at, points, centers),
        [SM, VM, VM],
        scratch=[ca],
        flops=FILL,
    )
    k1, fit = call(
        both_first_body,
        (kernel, sums),
        (at, pa, centers, vs[0], us[0], k0),
        [SM] + [VM] * 5,
        scratch=[ca],
        flops=FILL,
    )
    ks = [k0, k1]
    for k in (1, 2):
        more, fit = call(
            functools.partial(both_body, k),
            (kernel, sums),
            (at, pa, centers, vs[k], us[k], ks[k], fit),
            [SM] + [VM] * 6,
            scratch=[ca],
            flops=FILL,
        )
        ks.append(more)
    fitted = call(
        fit_body,
        sds((64, here), bf16),
        (vs[3], us[3], ks[3], fit),
        scratch=[pltpu.VMEM((here, 64), f32)],
        flops=FILL // 2,
    )
    block = sds((2, 4, 4, 8, 256), f32)
    got = []
    for k in (2, 1, 3, 0):
        own, other = call(normal_body, (block, block), (fitted, ks[k]), flops=FILL // 2)
        other = swap(other)
        if k:
            x = call(add_body, sds(block.shape, bf16), (own, other))
            got.append(across(x, k))
    x = call(gather_body, sds(block.shape, bf16), (own, other, *got))
    x = exchange(x.reshape(32, 8, 256), FACE)
    own, other = call(
        back_outer_body,
        (sds((16, 8, 256), f32), sds((16, 8, 256), f32)),
        (at, x, outer_factor),
        [SM] + [VM] * 2,
    )
    x = call(add_body, sds((16, 8, 256), f32), (own, swap(other)))
    x = exchange(x, LINE)
    own, other = call(
        functools.partial(back_inner_body, count),
        (sds((16, 8, 384), f32), sds((16, 8, 384), f32)),
        (at, x, inner_factor, term, full, residual),
        [SM] + [VM] * 5,
    )
    x = call(add_body, sds((16, 8, 384), f32), (own, swap(other)))
    x = exchange(x, LINE)
    keep, x = call(
        step_body, (sds((8, 384), f32), sds((32, 128), f32)), (at, x, residual), [SM, VM, VM]
    )
    x = exchange(x, ROW)
    x = call(beta_body, sds((8, 8, 384), f32), (x, keep))
    x = exchange(x, ("zh", "y"))
    out = sds((64, 256), f32)
    return call(final_body, (out, out, out), (x, iterate, direction))


def solution(mesh):
    fine = Mesh(mesh.devices.reshape(2, 4, 4, 4, 2), ("zh", "y", "zl", "x", "c"))
    placed = (
        P(ALL, None),
        P(),
        P(ROW, None),
        P(ROW, None),
        P(None, ROW),
        P(None, ROW),
        P(None, ROW),
    )
    return jax.shard_map(
        iteration,
        mesh=fine,
        in_specs=placed,
        out_specs=(P(None, ROW),) * 3,
        check_vma=False,
    )
```

```python
import functools
import jax
import jax.numpy as jnp
from jax import lax
from jax.sharding import Mesh, PartitionSpec as P
from jax.experimental import pallas as pl
from jax.experimental.pallas import tpu as pltpu

ridge_weight = 0.5
bf16, f32 = jnp.bfloat16, jnp.float32
ROW = ("zl", "x", "c")
LINE = ("zl", "x")
SIDE = ("y", "zl")
FACE = ("zh", "y", "zl")
ALL = ("zh", "y") + ROW
SWAP = [(0, 1), (1, 0)]
LOG2E = 1.4426950408889634
MIB = 1024 * 1024
FILL = 4_000_000_000
LAST = (((1,), (1,)), ((), ()))
VM = pl.BlockSpec(memory_space=pltpu.VMEM)
SM = pl.BlockSpec(memory_space=pltpu.SMEM)


def call(body, outs, args, specs=None, scratch=(), vmem=10, flops=0):
    return pl.pallas_call(
        body,
        out_shape=outs,
        in_specs=specs or [VM] * len(args),
        out_specs=jax.tree.map(lambda _: VM, outs),
        scratch_shapes=scratch,
        compiler_params=pltpu.CompilerParams(vmem_limit_bytes=vmem * MIB),
        cost_estimate=pl.CostEstimate(flops=flops, bytes_accessed=0, transcendentals=0),
    )(*args)


def sds(shape, dtype):
    return jax.ShapeDtypeStruct(shape, dtype)


def exchange(v, axes):
    return lax.all_to_all(v, axes, 0, 0, tiled=True)


def own_rows(at_ref, ref):
    return ref[pl.ds(pl.multiple_of(at_ref[0] * 16, 16), 16), :]


def eight_rows(at_ref, ref):
    start = at_ref[0] * 16 + at_ref[3] * 8
    return ref[pl.ds(pl.multiple_of(start, 8), 8), :]


def columns(at_ref, z, which):
    c = at_ref[1]
    return pl.ds(pl.multiple_of((2 * z + (c if which == 0 else 1 - c)) * 256, 256), 256)


def spread(value, ref):
    for r in range(ref.shape[0]):
        ref[r] = value


def prep_body(at_ref, d_ref, out_ref):
    d = own_rows(at_ref, d_ref)
    hi = d.astype(bf16)
    lo = (d - hi.astype(f32)).astype(bf16)
    out_ref[...] = jnp.concatenate([hi, lo], axis=0)


def rows_dot(at_ref, x_ref, y_ref, f_ref):
    acc = None
    for which, ref in ((0, x_ref), (1, y_ref)):
        for z in range(ref.shape[0]):
            part = lax.dot_general(
                ref[z], f_ref[:, columns(at_ref, z, which)], LAST, preferred_element_type=f32
            )
            acc = part if acc is None else acc + part
    return acc


def inner_body(at_ref, *refs):
    f_ref, term_ref, full_ref, out_ref = refs[8:]
    acc = None
    for which in range(2):
        for k in range(4):
            ref = refs[which * 4 + k]
            for m in range(4):
                z = (at_ref[4] ^ m) * 4 + (at_ref[2] ^ k)
                part = lax.dot_general(
                    ref[m], f_ref[:, columns(at_ref, z, which)], LAST, preferred_element_type=f32
                )
                acc = part if acc is None else acc + part
    term_ref[...] = acc[:16]
    full_ref[...] = acc[:16] + acc[16:]
    spread(acc[:16].astype(bf16), out_ref)


def stack_body(a_ref, b_ref, c_ref, d_ref, out_ref):
    for m, ref in enumerate((a_ref, b_ref, c_ref, d_ref)):
        out_ref[m] = ref[...]


def outer_body(at_ref, x_ref, y_ref, f_ref, out_ref):
    spread(rows_dot(at_ref, x_ref, y_ref, f_ref).astype(bf16), out_ref)


def norm_lanes(rows, first):
    wide = rows.astype(f32)
    lane = lax.broadcasted_iota(jnp.int32, (1, 128), 1)
    norm = jnp.sum(wide * wide, axis=1, keepdims=True) * -0.5
    one = norm.astype(bf16).astype(f32)
    rest = norm - one
    two = rest.astype(bf16).astype(f32)
    three = rest - two
    a, b = (0, 3) if first else (3, 0)
    ones = jnp.where((lane >= b) & (lane < b + 3), 1.0, 0.0)
    out = jnp.where(lane == a + 2, three, ones)
    out = jnp.where(lane == a + 1, two, out)
    return jnp.where(lane == a, one, out).astype(bf16)


def chunks(at_ref, shift, pa_ref, cen_ref, ca_ref, k_ref, fit=None):
    step = 256

    def load(i, slot):
        z = i * 4 + (at_ref[2] ^ shift)
        for h in range(2):
            cols = slice(h * 256, h * 256 + 256)
            block = cen_ref[columns(at_ref, z, h), :]
            ca_ref[slot, cols, :128] = block
            ca_ref[slot, cols, 128:] = norm_lanes(block, False)

    load(0, 0)

    def two(j, carry):
        for slot in range(2):
            i = j * 2 + slot
            load(jnp.minimum(i + 1, 3), 1 - slot)
            w = None if fit is None else fit.weights(i)
            for r in range(pa_ref.shape[0] // step):
                rows = pl.ds(r * step, step)
                if fit is not None:
                    fit.add(w, i, rows)
                for h in range(2):
                    cols = slice(h * 256, h * 256 + 256)
                    d = lax.dot_general(
                        pa_ref[rows, :], ca_ref[slot, cols, :], LAST, preferred_element_type=f32
                    )
                    k_ref[i, rows, cols] = jnp.exp2(d * (LOG2E * 8.0 / 128.0)).astype(bf16)
        return carry

    lax.fori_loop(0, 2, two, 0)


def augment_body(p_ref, pa_ref):
    pa_ref[:, :128] = p_ref[...]

    def block(r, carry):
        rows = pl.ds(pl.multiple_of(r * 512, 512), 512)
        pa_ref[rows, 128:] = norm_lanes(p_ref[rows, :], True)
        return carry

    lax.fori_loop(0, p_ref.shape[0] // 512, block, 0)


def fill_body(at_ref, pa_ref, cen_ref, k_ref, ca_ref):
    chunks(at_ref, 0, pa_ref, cen_ref, ca_ref, k_ref)


class Fitter:
    def __init__(self, v_ref, u_ref, k_ref, sum_ref):
        self.refs = v_ref, u_ref, k_ref, sum_ref

    def weights(self, i):
        v_ref, u_ref = self.refs[:2]
        return jnp.concatenate(
            [v_ref[:, i, :, :].reshape(64, 256), u_ref[:, i, :, :].reshape(64, 256)], axis=1
        )

    def add(self, w, i, rows):
        k_ref, sum_ref = self.refs[2:]
        sum_ref[rows, :] += lax.dot_general(
            k_ref[i, rows, :], w, LAST, preferred_element_type=f32
        )


def both_body(shift, at_ref, pa_ref, cen_ref, v_ref, u_ref, k_ref, old_ref, next_ref, sum_ref, ca_ref):
    sum_ref[...] = old_ref[...]
    fit = Fitter(v_ref, u_ref, k_ref, sum_ref)
    chunks(at_ref, shift + 1, pa_ref, cen_ref, ca_ref, next_ref, fit)


def both_first_body(at_ref, pa_ref, cen_ref, v_ref, u_ref, k_ref, next_ref, sum_ref, ca_ref):
    sum_ref[...] = jnp.zeros_like(sum_ref)
    fit = Fitter(v_ref, u_ref, k_ref, sum_ref)
    chunks(at_ref, 1, pa_ref, cen_ref, ca_ref, next_ref, fit)


def fit_body(v_ref, u_ref, k_ref, old_ref, out_ref, sum_ref):
    sum_ref[...] = old_ref[...]
    fit = Fitter(v_ref, u_ref, k_ref, sum_ref)

    def chunk(i, carry):
        w = fit.weights(i)
        for r in range(k_ref.shape[1] // 256):
            fit.add(w, i, pl.ds(r * 256, 256))
        return carry

    lax.fori_loop(0, k_ref.shape[0], chunk, 0)
    out_ref[...] = sum_ref[...].T.astype(bf16)


def normal_body(fit_ref, k_ref, own_ref, oth_ref):
    fitted = fit_ref[...]

    def chunk(i, carry):
        for h, ref in ((0, own_ref), (1, oth_ref)):
            n = jnp.dot(fitted, k_ref[i, :, h * 256 : h * 256 + 256], preferred_element_type=f32)
            n = n.reshape(4, 2, 8, 256)
            ref[0, :, i, :, :] = n[:, 0]
            ref[1, :, i, :, :] = n[:, 1]
        return carry

    lax.fori_loop(0, k_ref.shape[0], chunk, 0, unroll=2)


def add_body(a_ref, b_ref, out_ref):
    out_ref[...] = (a_ref[...] + b_ref[...].astype(f32)).astype(out_ref.dtype)


def sum_blocks(ref):
    parts = [ref[r].astype(f32) for r in range(ref.shape[0])]
    while len(parts) > 1:
        parts = [a + b for a, b in zip(parts[::2], parts[1::2])]
    return parts[0]


def gather_body(a_ref, b_ref, c_ref, d_ref, e_ref, out_ref):
    total = (
        (a_ref[...] + b_ref[...])
        + (c_ref[...].astype(f32) + d_ref[...].astype(f32))
        + e_ref[...].astype(f32)
    )
    out_ref[...] = total.astype(out_ref.dtype)


def back_outer_body(at_ref, x_ref, f_ref, own_ref, oth_ref):
    half = sum_blocks(x_ref).astype(bf16)
    for which, ref in ((0, own_ref), (1, oth_ref)):
        for z in range(ref.shape[0]):
            ref[z] = jnp.dot(half, f_ref[:, columns(at_ref, z, which)], preferred_element_type=f32)


def back_inner_body(count, at_ref, x_ref, f_ref, term_ref, full_ref, res_ref, own_ref, oth_ref):
    mine = pl.ds(pl.multiple_of(at_ref[3] * 8, 8), 8)
    shaped = sum_blocks(x_ref) / count + ridge_weight * term_ref[mine, :]
    half = shaped.astype(bf16)
    curve = jnp.sum(half.astype(f32) * full_ref[mine, :], axis=1, keepdims=True)
    res = eight_rows(at_ref, res_ref)
    old = jnp.sum(res * res, axis=1, keepdims=True)
    lane = lax.broadcasted_iota(jnp.int32, (8, 128), 1)
    extra = jnp.where(lane == 0, curve, old)
    for which, ref in ((0, own_ref), (1, oth_ref)):
        for z in range(ref.shape[0]):
            ref[z, :, :256] = jnp.dot(
                half, f_ref[:, columns(at_ref, z, which)], preferred_element_type=f32
            )
            ref[z, :, 256:] = extra


def diagonal():
    lane = lax.broadcasted_iota(jnp.int32, (8, 128), 1)
    return lane == lax.broadcasted_iota(jnp.int32, (8, 128), 0)


def step_body(at_ref, x_ref, res_ref, keep_ref, out_ref):
    block = sum_blocks(x_ref)
    curve, old = block[:, 256:257], block[:, 257:258]
    alpha = old / curve
    new = eight_rows(at_ref, res_ref) - alpha * block[:, :256]
    lane = lax.broadcasted_iota(jnp.int32, (8, 128), 1)
    keep_ref[:, :256] = new
    keep_ref[:, 256:] = jnp.where(lane == 0, alpha, old)
    part = jnp.sum(new * new, axis=1, keepdims=True)
    row = jnp.sum(jnp.where(diagonal(), part, 0.0), axis=0, keepdims=True)
    out_ref[...] = jnp.broadcast_to(row, out_ref.shape)


def beta_body(x_ref, keep_ref, out_ref):
    lane = lax.broadcasted_iota(jnp.int32, (8, 128), 1)
    row = jnp.sum(x_ref[...], axis=0, keepdims=True)
    total = jnp.sum(jnp.where(diagonal(), row, 0.0), axis=1, keepdims=True)
    extra = keep_ref[:, 256:]
    extra = jnp.where(lane == 0, extra, total / extra[:, 1:2])
    for r in range(out_ref.shape[0]):
        out_ref[r, :, :256] = keep_ref[:, :256]
        out_ref[r, :, 256:] = extra


def final_body(x_ref, it_ref, d_ref, ni_ref, nr_ref, nd_ref):
    for g in range(x_ref.shape[0]):
        start = (g % 4) * 16 + (g // 4) * 8
        rows = slice(start, start + 8)
        new = x_ref[g, :, :256]
        d = d_ref[rows, :]
        ni_ref[rows, :] = it_ref[rows, :] + x_ref[g, :, 256:257] * d
        nr_ref[rows, :] = new
        nd_ref[rows, :] = new + x_ref[g, :, 257:258] * d


def iteration(points, centers, inner_factor, outer_factor, iterate, residual, direction):
    at = jnp.stack([lax.axis_index(n) for n in ("y", "c", "x", "zh", "zl")])
    here = points.shape[0]
    count = float(here * 256)

    def swap(v):
        return lax.ppermute(v, "c", SWAP)

    def across(v, k):
        return lax.ppermute(v, "x", [(i, i ^ k) for i in range(4)])

    ca = pltpu.VMEM((2, 512, 256), bf16)
    kernel = sds((4, here, 512), bf16)
    sums = sds((here, 64), f32)
    x = call(prep_body, sds((32, 256), bf16), (at, direction), [SM, VM])
    line = [x]
    for k in (1, 2, 3):
        line.append(lax.ppermute(x, "zl", [(i, i ^ k) for i in range(4)]))
    pa = call(augment_body, sds((here, 256), bf16), (points,), flops=FILL // 4)
    x = call(stack_body, sds((4, 32, 256), bf16), line)
    mine = [x]
    for k in (1, 2, 3):
        mine.append(across(x, k))
    k0 = call(fill_body, kernel, (at, pa, centers), [SM, VM, VM], scratch=[ca], flops=FILL)
    term, full, x = call(
        inner_body,
        (sds((16, 256), f32), sds((16, 256), f32), sds((16, 16, 256), bf16)),
        (at, *mine, *[swap(v) for v in mine], inner_factor),
        [SM] + [VM] * 9,
    )
    x = exchange(x, LINE)
    x = call(outer_body, sds((16, 16, 256), bf16), (at, x, swap(x), outer_factor), [SM] + [VM] * 3)
    v = exchange(x, SIDE).reshape(4, 4, 16, 256)
    vs = [v] + [across(v, k) for k in (1, 2, 3)]
    us = [swap(v) for v in vs]
    k1, fit = call(
        both_first_body,
        (kernel, sums),
        (at, pa, centers, vs[0], us[0], k0),
        [SM] + [VM] * 5,
        scratch=[ca],
        flops=FILL,
    )
    ks = [k0, k1]
    for k in (1, 2):
        more, fit = call(
            functools.partial(both_body, k),
            (kernel, sums),
            (at, pa, centers, vs[k], us[k], ks[k], fit),
            [SM] + [VM] * 6,
            scratch=[ca],
            flops=FILL,
        )
        ks.append(more)
    fitted = call(
        fit_body,
        sds((64, here), bf16),
        (vs[3], us[3], ks[3], fit),
        scratch=[pltpu.VMEM((here, 64), f32)],
        flops=FILL // 2,
    )
    block = sds((2, 4, 4, 8, 256), f32)
    got = []
    for k in (2, 1, 3, 0):
        own, other = call(normal_body, (block, block), (fitted, ks[k]), flops=FILL // 2)
        other = swap(other)
        if k:
            x = call(add_body, sds(block.shape, bf16), (own, other))
            got.append(across(x, k))
    x = call(gather_body, sds(block.shape, bf16), (own, other, *got))
    x = exchange(x.reshape(32, 8, 256), FACE)
    own, other = call(
        back_outer_body,
        (sds((16, 8, 256), f32), sds((16, 8, 256), f32)),
        (at, x, outer_factor),
        [SM] + [VM] * 2,
    )
    x = call(add_body, sds((16, 8, 256), f32), (own, swap(other)))
    x = exchange(x, LINE)
    own, other = call(
        functools.partial(back_inner_body, count),
        (sds((16, 8, 384), f32), sds((16, 8, 384), f32)),
        (at, x, inner_factor, term, full, residual),
        [SM] + [VM] * 5,
    )
    x = call(add_body, sds((16, 8, 384), f32), (own, swap(other)))
    x = exchange(x, LINE)
    keep, x = call(
        step_body, (sds((8, 384), f32), sds((32, 128), f32)), (at, x, residual), [SM, VM, VM]
    )
    x = exchange(x, ROW)
    x = call(beta_body, sds((8, 8, 384), f32), (x, keep))
    x = exchange(x, ("zh", "y"))
    out = sds((64, 256), f32)
    return call(final_body, (out, out, out), (x, iterate, direction))


def solution(mesh):
    fine = Mesh(mesh.devices.reshape(2, 4, 4, 4, 2), ("zh", "y", "zl", "x", "c"))
    placed = (
        P(ALL, None),
        P(),
        P(ROW, None),
        P(ROW, None),
        P(None, ROW),
        P(None, ROW),
        P(None, ROW),
    )
    return jax.shard_map(
        iteration,
        mesh=fine,
        in_specs=placed,
        out_specs=(P(None, ROW),) * 3,
        check_vma=False,
    )
```

```python
import functools
import jax
import jax.numpy as jnp
from jax import lax
from jax.sharding import Mesh, PartitionSpec as P
from jax.experimental import pallas as pl
from jax.experimental.pallas import tpu as pltpu

ridge_weight = 0.5
bf16, f32 = jnp.bfloat16, jnp.float32
ROW = ("zl", "x", "c")
LINE = ("zl", "x")
SIDE = ("y", "zl")
FACE = ("zh", "y", "zl")
ALL = ("zh", "y") + ROW
SWAP = [(0, 1), (1, 0)]
LOG2E = 1.4426950408889634
MIB = 1024 * 1024
FILL = 4_000_000_000
LAST = (((1,), (1,)), ((), ()))
VM = pl.BlockSpec(memory_space=pltpu.VMEM)
SM = pl.BlockSpec(memory_space=pltpu.SMEM)
HB = pl.BlockSpec(memory_space=pltpu.HBM)


def call(body, outs, args, specs=None, scratch=(), vmem=10, flops=0):
    return pl.pallas_call(
        body,
        out_shape=outs,
        in_specs=specs or [VM] * len(args),
        out_specs=jax.tree.map(lambda _: VM, outs),
        scratch_shapes=scratch,
        compiler_params=pltpu.CompilerParams(vmem_limit_bytes=vmem * MIB),
        cost_estimate=pl.CostEstimate(flops=flops, bytes_accessed=0, transcendentals=0),
    )(*args)


def sds(shape, dtype):
    return jax.ShapeDtypeStruct(shape, dtype)


def exchange(v, axes):
    return lax.all_to_all(v, axes, 0, 0, tiled=True)


def own_rows(at_ref, ref):
    return ref[pl.ds(pl.multiple_of(at_ref[0] * 16, 16), 16), :]


def eight_rows(at_ref, ref):
    start = at_ref[0] * 16 + at_ref[3] * 8
    return ref[pl.ds(pl.multiple_of(start, 8), 8), :]


def columns(at_ref, z, which):
    c = at_ref[1]
    return pl.ds(pl.multiple_of((2 * z + (c if which == 0 else 1 - c)) * 256, 256), 256)


def spread(value, ref):
    for r in range(ref.shape[0]):
        ref[r] = value


def prep_body(at_ref, d_ref, out_ref):
    d = own_rows(at_ref, d_ref)
    hi = d.astype(bf16)
    lo = (d - hi.astype(f32)).astype(bf16)
    out_ref[...] = jnp.concatenate([hi, lo], axis=0)


def rows_dot(at_ref, x_ref, y_ref, f_ref):
    acc = None
    for which, ref in ((0, x_ref), (1, y_ref)):
        for z in range(ref.shape[0]):
            part = lax.dot_general(
                ref[z], f_ref[:, columns(at_ref, z, which)], LAST, preferred_element_type=f32
            )
            acc = part if acc is None else acc + part
    return acc


def inner_body(at_ref, *refs):
    f_ref, term_ref, full_ref, out_ref = refs[8:]
    acc = None
    for which in range(2):
        for k in range(4):
            ref = refs[which * 4 + k]
            for m in range(4):
                z = (at_ref[4] ^ m) * 4 + (at_ref[2] ^ k)
                part = lax.dot_general(
                    ref[m], f_ref[:, columns(at_ref, z, which)], LAST, preferred_element_type=f32
                )
                acc = part if acc is None else acc + part
    term_ref[...] = acc[:16]
    full_ref[...] = acc[:16] + acc[16:]
    spread(acc[:16].astype(bf16), out_ref)


def stack_body(a_ref, b_ref, c_ref, d_ref, out_ref):
    for m, ref in enumerate((a_ref, b_ref, c_ref, d_ref)):
        out_ref[m] = ref[...]


def outer_body(at_ref, x_ref, y_ref, f_ref, out_ref):
    spread(rows_dot(at_ref, x_ref, y_ref, f_ref).astype(bf16), out_ref)


def norm_lanes(rows, first):
    wide = rows.astype(f32)
    lane = lax.broadcasted_iota(jnp.int32, (1, 128), 1)
    norm = jnp.sum(wide * wide, axis=1, keepdims=True) * -0.5
    one = norm.astype(bf16).astype(f32)
    rest = norm - one
    two = rest.astype(bf16).astype(f32)
    three = rest - two
    a, b = (0, 3) if first else (3, 0)
    ones = jnp.where((lane >= b) & (lane < b + 3), 1.0, 0.0)
    out = jnp.where(lane == a + 2, three, ones)
    out = jnp.where(lane == a + 1, two, out)
    return jnp.where(lane == a, one, out).astype(bf16)


def chunks(at_ref, shift, pa_ref, cen_ref, ca_ref, k_ref, fit=None, landed=None):
    step = 256

    def load(i, slot):
        z = i * 4 + (at_ref[2] ^ shift)
        for h in range(2):
            cols = slice(h * 256, h * 256 + 256)
            block = cen_ref[columns(at_ref, z, h), :] if landed is None else cen_ref[i * 2 + h]
            ca_ref[slot, cols, :128] = block
            ca_ref[slot, cols, 128:] = norm_lanes(block, False)

    load(0, 0)
    for copy in landed or ():
        copy.wait()

    def two(j, carry):
        for slot in range(2):
            i = j * 2 + slot
            load(jnp.minimum(i + 1, 3), 1 - slot)
            w = None if fit is None else fit.weights(i)
            for r in range(pa_ref.shape[0] // step):
                rows = pl.ds(r * step, step)
                if fit is not None:
                    fit.add(w, i, rows)
                for h in range(2):
                    cols = slice(h * 256, h * 256 + 256)
                    d = lax.dot_general(
                        pa_ref[rows, :], ca_ref[slot, cols, :], LAST, preferred_element_type=f32
                    )
                    k_ref[i, rows, cols] = jnp.exp2(d * (LOG2E * 8.0 / 128.0)).astype(bf16)
        return carry

    lax.fori_loop(0, 2, two, 0)


def augment_body(hbm_ref, pa_ref, p_ref, sem):
    part = p_ref.shape[0] // sem.shape[0]
    copies = []
    for q in range(sem.shape[0]):
        rows = pl.ds(q * part, part)
        copies.append(pltpu.make_async_copy(hbm_ref.at[rows, :], p_ref.at[rows, :], sem.at[q]))
        copies[q].start()
    for copy in copies:
        copy.wait()

    def block(q, carry):
        rows = pl.ds(pl.multiple_of(q * part, part), part)
        pa_ref[rows, :128] = p_ref[rows, :]
        pa_ref[rows, 128:] = norm_lanes(p_ref[rows, :], True)
        return carry

    lax.fori_loop(0, sem.shape[0], block, 0)


def fill_body(at_ref, pa_ref, hbm_ref, k_ref, ca_ref, cen_ref, sem):
    copies = []
    for i in range(4):
        for h in range(2):
            rows = columns(at_ref, i * 4 + at_ref[2], h)
            n = i * 2 + h
            copies.append(pltpu.make_async_copy(hbm_ref.at[rows, :], cen_ref.at[n], sem.at[n]))
            copies[n].start()
    for copy in copies[:2]:
        copy.wait()
    chunks(at_ref, 0, pa_ref, cen_ref, ca_ref, k_ref, landed=copies[2:])


class Fitter:
    def __init__(self, v_ref, u_ref, k_ref, sum_ref):
        self.refs = v_ref, u_ref, k_ref, sum_ref

    def weights(self, i):
        v_ref, u_ref = self.refs[:2]
        return jnp.concatenate(
            [v_ref[:, i, :, :].reshape(64, 256), u_ref[:, i, :, :].reshape(64, 256)], axis=1
        )

    def add(self, w, i, rows):
        k_ref, sum_ref = self.refs[2:]
        sum_ref[rows, :] += lax.dot_general(
            k_ref[i, rows, :], w, LAST, preferred_element_type=f32
        )


def both_body(shift, at_ref, pa_ref, cen_ref, v_ref, u_ref, k_ref, old_ref, next_ref, sum_ref, ca_ref):
    sum_ref[...] = old_ref[...]
    fit = Fitter(v_ref, u_ref, k_ref, sum_ref)
    chunks(at_ref, shift + 1, pa_ref, cen_ref, ca_ref, next_ref, fit)


def both_first_body(at_ref, pa_ref, cen_ref, v_ref, u_ref, k_ref, next_ref, sum_ref, ca_ref):
    sum_ref[...] = jnp.zeros_like(sum_ref)
    fit = Fitter(v_ref, u_ref, k_ref, sum_ref)
    chunks(at_ref, 1, pa_ref, cen_ref, ca_ref, next_ref, fit)


def fit_body(v_ref, u_ref, k_ref, old_ref, out_ref, sum_ref):
    sum_ref[...] = old_ref[...]
    fit = Fitter(v_ref, u_ref, k_ref, sum_ref)

    def chunk(i, carry):
        w = fit.weights(i)
        for r in range(k_ref.shape[1] // 256):
            fit.add(w, i, pl.ds(r * 256, 256))
        return carry

    lax.fori_loop(0, k_ref.shape[0], chunk, 0)
    out_ref[...] = sum_ref[...].T.astype(bf16)


def normal_body(fit_ref, k_ref, own_ref, oth_ref):
    fitted = fit_ref[...]

    def chunk(i, carry):
        for h, ref in ((0, own_ref), (1, oth_ref)):
            n = jnp.dot(fitted, k_ref[i, :, h * 256 : h * 256 + 256], preferred_element_type=f32)
            n = n.reshape(4, 2, 8, 256)
            ref[0, :, i, :, :] = n[:, 0]
            ref[1, :, i, :, :] = n[:, 1]
        return carry

    lax.fori_loop(0, k_ref.shape[0], chunk, 0, unroll=2)


def add_body(a_ref, b_ref, out_ref):
    out_ref[...] = (a_ref[...] + b_ref[...].astype(f32)).astype(out_ref.dtype)


def sum_blocks(ref):
    parts = [ref[r].astype(f32) for r in range(ref.shape[0])]
    while len(parts) > 1:
        parts = [a + b for a, b in zip(parts[::2], parts[1::2])]
    return parts[0]


def gather_body(a_ref, b_ref, c_ref, d_ref, e_ref, out_ref):
    total = (
        (a_ref[...] + b_ref[...])
        + (c_ref[...].astype(f32) + d_ref[...].astype(f32))
        + e_ref[...].astype(f32)
    )
    out_ref[...] = total.astype(out_ref.dtype)


def back_outer_body(at_ref, x_ref, f_ref, own_ref, oth_ref):
    half = sum_blocks(x_ref).astype(bf16)
    for which, ref in ((0, own_ref), (1, oth_ref)):
        for z in range(ref.shape[0]):
            ref[z] = jnp.dot(half, f_ref[:, columns(at_ref, z, which)], preferred_element_type=f32)


def back_inner_body(count, at_ref, x_ref, f_ref, term_ref, full_ref, res_ref, own_ref, oth_ref):
    mine = pl.ds(pl.multiple_of(at_ref[3] * 8, 8), 8)
    shaped = sum_blocks(x_ref) / count + ridge_weight * term_ref[mine, :]
    half = shaped.astype(bf16)
    curve = jnp.sum(half.astype(f32) * full_ref[mine, :], axis=1, keepdims=True)
    res = eight_rows(at_ref, res_ref)
    old = jnp.sum(res * res, axis=1, keepdims=True)
    lane = lax.broadcasted_iota(jnp.int32, (8, 128), 1)
    extra = jnp.where(lane == 0, curve, old)
    for which, ref in ((0, own_ref), (1, oth_ref)):
        for z in range(ref.shape[0]):
            ref[z, :, :256] = jnp.dot(
                half, f_ref[:, columns(at_ref, z, which)], preferred_element_type=f32
            )
            ref[z, :, 256:] = extra


def diagonal():
    lane = lax.broadcasted_iota(jnp.int32, (8, 128), 1)
    return lane == lax.broadcasted_iota(jnp.int32, (8, 128), 0)


def step_body(at_ref, x_ref, res_ref, keep_ref, out_ref):
    block = sum_blocks(x_ref)
    curve, old = block[:, 256:257], block[:, 257:258]
    alpha = old / curve
    new = eight_rows(at_ref, res_ref) - alpha * block[:, :256]
    lane = lax.broadcasted_iota(jnp.int32, (8, 128), 1)
    keep_ref[:, :256] = new
    keep_ref[:, 256:] = jnp.where(lane == 0, alpha, old)
    part = jnp.sum(new * new, axis=1, keepdims=True)
    row = jnp.sum(jnp.where(diagonal(), part, 0.0), axis=0, keepdims=True)
    out_ref[...] = jnp.broadcast_to(row, out_ref.shape)


def beta_body(x_ref, keep_ref, out_ref):
    lane = lax.broadcasted_iota(jnp.int32, (8, 128), 1)
    row = jnp.sum(x_ref[...], axis=0, keepdims=True)
    total = jnp.sum(jnp.where(diagonal(), row, 0.0), axis=1, keepdims=True)
    extra = keep_ref[:, 256:]
    extra = jnp.where(lane == 0, extra, total / extra[:, 1:2])
    for r in range(out_ref.shape[0]):
        out_ref[r, :, :256] = keep_ref[:, :256]
        out_ref[r, :, 256:] = extra


def final_body(x_ref, it_ref, d_ref, ni_ref, nr_ref, nd_ref):
    for g in range(x_ref.shape[0]):
        start = (g % 4) * 16 + (g // 4) * 8
        rows = slice(start, start + 8)
        new = x_ref[g, :, :256]
        d = d_ref[rows, :]
        ni_ref[rows, :] = it_ref[rows, :] + x_ref[g, :, 256:257] * d
        nr_ref[rows, :] = new
        nd_ref[rows, :] = new + x_ref[g, :, 257:258] * d


def iteration(points, centers, inner_factor, outer_factor, iterate, residual, direction):
    at = jnp.stack([lax.axis_index(n) for n in ("y", "c", "x", "zh", "zl")])
    here = points.shape[0]
    count = float(here * 256)

    def swap(v):
        return lax.ppermute(v, "c", SWAP)

    def across(v, k):
        return lax.ppermute(v, "x", [(i, i ^ k) for i in range(4)])

    ca = pltpu.VMEM((2, 512, 256), bf16)
    kernel = sds((4, here, 512), bf16)
    sums = sds((here, 64), f32)
    x = call(prep_body, sds((32, 256), bf16), (at, direction), [SM, VM])
    line = [x]
    for k in (1, 2, 3):
        line.append(lax.ppermute(x, "zl", [(i, i ^ k) for i in range(4)]))
    pa = call(
        augment_body,
        sds((here, 256), bf16),
        (pltpu.with_memory_space_constraint(points, pltpu.HBM),),
        [HB],
        scratch=[pltpu.VMEM(points.shape, bf16), pltpu.SemaphoreType.DMA((4,))],
        flops=FILL // 4,
    )
    x = call(stack_body, sds((4, 32, 256), bf16), line)
    mine = [x]
    for k in (1, 2, 3):
        mine.append(across(x, k))
    k0 = call(
        fill_body,
        kernel,
        (at, pa, pltpu.with_memory_space_constraint(centers, pltpu.HBM)),
        [SM, VM, HB],
        scratch=[ca, pltpu.VMEM((8, 256, 128), bf16), pltpu.SemaphoreType.DMA((8,))],
        flops=FILL,
    )
    term, full, x = call(
        inner_body,
        (sds((16, 256), f32), sds((16, 256), f32), sds((16, 16, 256), bf16)),
        (at, *mine, *[swap(v) for v in mine], inner_factor),
        [SM] + [VM] * 9,
    )
    x = exchange(x, LINE)
    x = call(outer_body, sds((16, 16, 256), bf16), (at, x, swap(x), outer_factor), [SM] + [VM] * 3)
    v = exchange(x, SIDE).reshape(4, 4, 16, 256)
    vs = [v] + [across(v, k) for k in (1, 2, 3)]
    us = [swap(v) for v in vs]
    k1, fit = call(
        both_first_body,
        (kernel, sums),
        (at, pa, centers, vs[0], us[0], k0),
        [SM] + [VM] * 5,
        scratch=[ca],
        flops=FILL,
    )
    ks = [k0, k1]
    for k in (1, 2):
        more, fit = call(
            functools.partial(both_body, k),
            (kernel, sums),
            (at, pa, centers, vs[k], us[k], ks[k], fit),
            [SM] + [VM] * 6,
            scratch=[ca],
            flops=FILL,
        )
        ks.append(more)
    fitted = call(
        fit_body,
        sds((64, here), bf16),
        (vs[3], us[3], ks[3], fit),
        scratch=[pltpu.VMEM((here, 64), f32)],
        flops=FILL // 2,
    )
    block = sds((2, 4, 4, 8, 256), f32)
    got = []
    for k in (2, 1, 3, 0):
        own, other = call(normal_body, (block, block), (fitted, ks[k]), flops=FILL // 2)
        other = swap(other)
        if k:
            x = call(add_body, sds(block.shape, bf16), (own, other))
            got.append(across(x, k))
    x = call(gather_body, sds(block.shape, bf16), (own, other, *got))
    x = exchange(x.reshape(32, 8, 256), FACE)
    own, other = call(
        back_outer_body,
        (sds((16, 8, 256), f32), sds((16, 8, 256), f32)),
        (at, x, outer_factor),
        [SM] + [VM] * 2,
    )
    x = call(add_body, sds((16, 8, 256), f32), (own, swap(other)))
    x = exchange(x, LINE)
    own, other = call(
        functools.partial(back_inner_body, count),
        (sds((16, 8, 384), f32), sds((16, 8, 384), f32)),
        (at, x, inner_factor, term, full, residual),
        [SM] + [VM] * 5,
    )
    x = call(add_body, sds((16, 8, 384), f32), (own, swap(other)))
    x = exchange(x, LINE)
    keep, x = call(
        step_body, (sds((8, 384), f32), sds((32, 128), f32)), (at, x, residual), [SM, VM, VM]
    )
    x = exchange(x, ROW)
    x = call(beta_body, sds((8, 8, 384), f32), (x, keep))
    x = exchange(x, ("zh", "y"))
    out = sds((64, 256), f32)
    return call(final_body, (out, out, out), (x, iterate, direction))


def solution(mesh):
    fine = Mesh(mesh.devices.reshape(2, 4, 4, 4, 2), ("zh", "y", "zl", "x", "c"))
    placed = (
        P(ALL, None),
        P(),
        P(ROW, None),
        P(ROW, None),
        P(None, ROW),
        P(None, ROW),
        P(None, ROW),
    )
    return jax.shard_map(
        iteration,
        mesh=fine,
        in_specs=placed,
        out_specs=(P(None, ROW),) * 3,
        check_vma=False,
    )
```
